32 devices in a mesh: img: 16 (over z, y, x), blk: 2 (over core).
Axes of the slice: x: 2, y: 2, z: 4, core: 2. Of those that a mesh axis runs over, the one named last changes fastest.
Arguments:
- descriptors: bfloat16 [64, 128, 256], P(('img', 'blk')), may hold values from -8 to 8
- covisible: int32 [64, 6], P(('img', 'blk')), may hold values from 0 to 63, as said below
- tile_counts: int32 [64], P(('img', 'blk')), may hold values from 1 to 6, as said below
- keypoints: int32 [64], replicated, may hold values from 32 to 128, as said below
- query_weight: bfloat16 [256, 256], replicated, may hold values from -0.375 to 0.375
- key_weight: bfloat16 [256, 256], replicated, may hold values from -0.375 to 0.375
- value_weight: bfloat16 [256, 256], replicated, may hold values from -0.375 to 0.375
- merge_weight: bfloat16 [512, 512], replicated, may hold values from -0.25 to 0.25
- output_weight: bfloat16 [512, 256], replicated, may hold values from -0.25 to 0.25
- dustbin: float32 [1], replicated, may hold values from 0.5 to 2
Outputs:
- plan: float32 [64, 6, 128, 128], P(('img', 'blk'))
- row_bin: float32 [64, 128], P(('img', 'blk'))
- col_bin: float32 [64, 128], P(('img', 'blk'))
The draws below stay inside these ranges and needn't reach their ends.
Inputs may be any that keep to these rules, and one draw needn't show every extreme that they name: `covisible`: the 6 entries of a block's row name different blocks, never the block itself, all within its own image group of 4 consecutive blocks or the groups just before and after it. `tile_counts`: some block uses all 6 of its listed blocks. The valid keypoints of a block are its first ones; some block is full.
All inputs are finite; a program needn't handle non-finite values.
Results may differ from the reference program's by a relative error of at most 0.0032.
Values may be sent and summed in bfloat16 or wider, within the bound.
A program may use at most 64 MiB of HBM per device.

```python
import math
import jax
import jax.numpy as jnp
from jax import lax

D = 256
HEADS = 4
BLOCK = 128
TILES = 6
ITERS = 3
GROUP = 4
NB = 64


def draw_descriptors(key, part):
    drawn_key = jax.random.fold_in(key, 101)
    return jnp.clip(jax.random.normal(drawn_key, (NB, BLOCK, D), jnp.float32), -8.0, 8.0).astype(jnp.bfloat16)


def draw_covisible(key, part):
    rows = jnp.arange(NB, dtype=jnp.int32)
    groups = rows // GROUP
    slots = jnp.arange(3 * GROUP, dtype=jnp.int32)
    candidate = (groups[:, None] - 1) * GROUP + slots[None, :]
    usable = (candidate >= 0) & (candidate < NB) & (candidate != rows[:, None])
    ranks = jax.vmap(lambda sub: jax.random.permutation(sub, 3 * GROUP))(jax.random.split(jax.random.fold_in(key, 201), NB))
    ranking = ranks.astype(jnp.int32) + jnp.where(usable, 0, 3 * GROUP)
    order = jnp.argsort(ranking, axis=1, stable=True)[:, :TILES]
    return jnp.take_along_axis(candidate, order, axis=1).astype(jnp.int32)


def draw_tile_counts(key, part):
    rows = jnp.arange(NB, dtype=jnp.int32)
    drawn = jax.random.randint(jax.random.fold_in(key, 301), (NB,), 1, TILES + 1)
    return jnp.where(rows % 5 == 0, TILES, drawn).astype(jnp.int32)


def draw_keypoints(key, part):
    rows = jnp.arange(NB, dtype=jnp.int32)
    drawn = jax.random.randint(jax.random.fold_in(key, 401), (NB,), BLOCK // 4, BLOCK + 1)
    return jnp.where(rows % 3 == 0, BLOCK, drawn).astype(jnp.int32)


def normal_values(rng, extent, spread, limit, held_as=jnp.bfloat16):
    return jnp.clip(spread * jax.random.normal(rng, extent, jnp.float32), -limit, limit).astype(held_as)


def setup_inputs(seed: int = 0) -> dict:
    splits = jax.random.split(jax.random.key(seed), 11)
    return {
        "descriptors": draw_descriptors(jax.random.fold_in(splits[10], 71), 0),
        "covisible": draw_covisible(jax.random.fold_in(splits[10], 71), 0),
        "tile_counts": draw_tile_counts(jax.random.fold_in(splits[10], 71), 0),
        "keypoints": draw_keypoints(jax.random.fold_in(splits[10], 71), 0),
        "query_weight": normal_values(splits[4], (D, D), D ** -0.5, 0.375),
        "key_weight": normal_values(splits[5], (D, D), D ** -0.5, 0.375),
        "value_weight": normal_values(splits[6], (D, D), D ** -0.5, 0.375),
        "merge_weight": normal_values(splits[7], (2 * D, 2 * D), (2 * D) ** -0.5, 0.25),
        "output_weight": normal_values(splits[8], (2 * D, D), (2 * D) ** -0.5, 0.25),
        "dustbin": jnp.clip(jax.random.uniform(splits[9], (1,), jnp.float32, 0.5, 2.0), 0.5, 2.0),
    }


def project_rows(values, weight):
    flat = jnp.dot(values.reshape(-1, values.shape[-1]), weight, preferred_element_type=jnp.float32)
    return flat.reshape(values.shape[:-1] + (weight.shape[1],)).astype(jnp.bfloat16)

def reference(descriptors, covisible, tile_counts, keypoints, query_weight, key_weight, value_weight, merge_weight, output_weight, dustbin):
    block_count, block_len, feature_dim = descriptors.shape
    head_dim = feature_dim // HEADS
    tile_count = covisible.shape[1]
    query = project_rows(descriptors, query_weight)
    keys_all = project_rows(descriptors, key_weight)
    values_all = project_rows(descriptors, value_weight)
    tile_slots = jnp.arange(tile_count, dtype=jnp.int32)
    positions = jnp.arange(block_len, dtype=jnp.int32)

    def attend(pieces):
        query_block, own_block, row_cols, count = pieces
        key_tiles = keys_all[row_cols].reshape(tile_count * block_len, HEADS, head_dim).astype(jnp.float32)
        value_tiles = values_all[row_cols].reshape(tile_count * block_len, HEADS, head_dim).astype(jnp.float32)
        key_live = (tile_slots[:, None] < count) & (positions[None, :] < keypoints[row_cols][:, None])
        logits = jnp.einsum('qhd,khd->hqk', query_block.reshape(block_len, HEADS, head_dim).astype(jnp.float32), key_tiles) / math.sqrt(head_dim)
        logits = jnp.where(key_live.reshape(1, 1, -1), logits, -1e+30)
        highest = lax.optimization_barrier(jnp.max(logits, axis=2, keepdims=True))
        weights = jnp.exp(logits - highest)
        weights = (weights / lax.optimization_barrier(jnp.sum(weights, axis=2, keepdims=True))).astype(jnp.bfloat16)
        message = jnp.einsum('hqk,khd->qhd', weights.astype(jnp.float32), value_tiles).reshape(block_len, feature_dim).astype(jnp.bfloat16)
        joined = jnp.concatenate([own_block, message], axis=1)
        hidden = jnp.maximum(jnp.dot(joined, merge_weight, preferred_element_type=jnp.float32), 0.0).astype(jnp.bfloat16)
        return (own_block.astype(jnp.float32) + jnp.dot(hidden, output_weight, preferred_element_type=jnp.float32)).astype(jnp.bfloat16)
    refined = lax.map(attend, (query, descriptors, covisible, tile_counts))

    def score_tiles(pieces):
        own_block, row_cols = pieces
        other = refined[row_cols].astype(jnp.float32)
        return jnp.einsum('id,kjd->kij', own_block.astype(jnp.float32), other) / math.sqrt(feature_dim)
    scores = lax.map(score_tiles, (refined, covisible))
    row_live = positions[None, :] < keypoints[:, None]
    tile_live = tile_slots[None, :] < tile_counts[:, None]
    col_live = row_live[covisible]
    valid = tile_live[:, :, None, None] & row_live[:, None, :, None] & col_live[:, :, None, :]
    dust = dustbin[0]
    col_pot = jnp.zeros((block_count, block_len), jnp.float32)
    row_pot = jnp.zeros((block_count, block_len), jnp.float32)
    for sweep in range(ITERS):
        tile_pot = col_pot[covisible]
        shifted = jnp.where(valid, scores + tile_pot[:, :, None, :], -1e+30)
        highest = jnp.maximum(lax.optimization_barrier(jnp.max(shifted, axis=(1, 3))), dust)
        total = lax.optimization_barrier(jnp.sum(jnp.exp(shifted - highest[:, None, :, None]), axis=(1, 3))) + jnp.exp(dust - highest)
        row_pot = -(highest + jnp.log(total))
        mass = lax.optimization_barrier(jnp.sum(jnp.where(valid, jnp.exp(scores + row_pot[:, None, :, None] + tile_pot[:, :, None, :]), 0.0), axis=2))
        col_sum = jax.ops.segment_sum(mass.reshape(block_count * tile_count, block_len), covisible.reshape(-1), num_segments=block_count)
        col_pot = col_pot - jnp.log(col_sum + jnp.exp(dust + col_pot))
    tile_pot = col_pot[covisible]
    plan = jnp.where(valid, scores + row_pot[:, None, :, None] + tile_pot[:, :, None, :], 0.0)
    row_bin = jnp.where(row_live, dust + row_pot, 0.0)
    col_bin = jnp.where(row_live, dust + col_pot, 0.0)
    return (plan, row_bin, col_bin)
```

```python
import functools
import math

import jax
import jax.numpy as jnp
from jax import lax
from jax.experimental import pallas as pl
from jax.experimental.pallas import tpu as pltpu
from jax.sharding import PartitionSpec as P

HEADS = 4
ITERS = 3
DEAD = -1e30
MESH = pl.DeviceIdType.MESH
VMEM_BYTES = 32 * 1024 * 1024


def kernel(
    img_count,
    blk_count,
    desc_in,
    cov_in,
    count_in,
    kpt_in,
    wq_in,
    wk_in,
    wv_in,
    wm_in,
    wo_in,
    dust_in,
    scores,
    tail_ref,
    desc_ref,
    cov_ref,
    count_ref,
    kpt_ref,
    wq_ref,
    wk_ref,
    wv_ref,
    wm_ref,
    wo_ref,
    dust_ref,
    load_sem,
    near_desc,
    near_ref,
    near_k,
    near_v,
    query,
    merged,
    acc,
    mass_in,
    pot,
    desc_ssem,
    desc_rsem,
    ref_ssem,
    ref_rsem,
    mass_ssem,
    mass_rsem,
):
    local, block, width = desc_ref.shape
    tiles = cov_ref.shape[1]
    group = local * blk_count
    head_dim = width // HEADS
    img = lax.axis_index("img")
    blk = lax.axis_index("blk")
    others = [lax.rem(blk + step, blk_count) for step in range(1, blk_count)]
    first_block = (img - 1) * group

    def exists(shift):
        if shift == 0:
            return True
        return img + shift < img_count if shift > 0 else img + shift >= 0

    def guarded(shift, body):
        if shift == 0:
            body()
        else:
            pl.when(exists(shift))(body)

    pairs = (
        (desc_in, desc_ref),
        (wq_in, wq_ref),
        (wk_in, wk_ref),
        (wv_in, wv_ref),
        (wm_in, wm_ref),
        (cov_in, cov_ref),
        (count_in, count_ref),
        (kpt_in, kpt_ref),
        (dust_in, dust_ref),
        (wo_in, wo_ref),
    )
    loads = [
        pltpu.make_async_copy(source, target, load_sem.at[place])
        for place, (source, target) in enumerate(pairs)
    ]

    barrier = pltpu.get_barrier_semaphore()
    for shift in range(-2, 3):
        def greet(shift=shift):
            for member in others if shift == 0 else range(blk_count):
                pl.semaphore_signal(
                    barrier, inc=1, device_id=(img + shift, member), device_id_type=MESH
                )
        guarded(shift, greet)

    for load in loads:
        load.start()

    def slot(near, section, member):
        return near.at[pl.ds((section * blk_count + member) * local, local)]

    def sender(source, near, ssem, rsem, section, shift, member):
        return pltpu.make_async_remote_copy(
            src_ref=source,
            dst_ref=slot(near, section, blk),
            send_sem=ssem.at[section, member],
            recv_sem=rsem.at[section, blk],
            device_id=(img + shift, member),
            device_id_type=MESH,
        )

    def arrival(near, ssem, rsem, section, member):
        here = slot(near, section, member)
        return pltpu.make_async_remote_copy(
            src_ref=here,
            dst_ref=here,
            send_sem=ssem.at[section, member],
            recv_sem=rsem.at[section, member],
            device_id=(img, others[0]),
            device_id_type=MESH,
        )

    def send_own(source, near, ssem, rsem):
        for shift in (1, -1):
            guarded(
                shift,
                lambda shift=shift: sender(
                    source, near, ssem, rsem, 1 - shift, shift, blk
                ).start(),
            )
        for member in others:
            sender(source, near, ssem, rsem, 1, 0, member).start()

    def relay(near, ssem, rsem, section):
        def body():
            arrival(near, ssem, rsem, section, blk).wait_recv()
            for member in others:
                sender(slot(near, section, blk), near, ssem, rsem, section, 0, member).start()
        guarded(section - 1, body)

    def wait_relayed(near, ssem, rsem, section, after=None):
        def body():
            for member in others:
                arrival(near, ssem, rsem, section, member).wait_recv()
                if after is not None:
                    after(section, member)
        guarded(section - 1, body)

    def drain(source, near, ssem, rsem):
        for shift in (1, -1):
            guarded(
                shift,
                lambda shift=shift: sender(
                    source, near, ssem, rsem, 1 - shift, shift, blk
                ).wait_send(),
            )
        for section in range(3):
            def body(section=section):
                for member in others:
                    sender(source, near, ssem, rsem, section, 0, member).wait_send()
            guarded(section - 1, body)

    def project(rows, section, member):
        where_to = pl.ds((section * blk_count + member) * local, local)
        for weight, target in ((wk_ref, near_k), (wv_ref, near_v)):
            out = jnp.dot(rows, weight[...], preferred_element_type=jnp.float32)
            target[where_to] = out.astype(jnp.bfloat16).reshape(local, block, width)

    def project_near(section, member):
        rows = near_desc[pl.ds((section * blk_count + member) * local, local)]
        project(rows.reshape(local * block, width), section, member)

    for source in range(-2, 3):
        if source != 0:
            @pl.when(jnp.logical_not(exists(source)))
            def _(source=source):
                for sweep in range(ITERS):
                    mass_in[sweep, source + 2] = jnp.zeros(mass_in.shape[2:], jnp.float32)

    low = jnp.maximum(img - 2, 0)
    high = jnp.minimum(img + 2, img_count - 1)
    pl.semaphore_wait(barrier, (high - low + 1) * blk_count - 1)
    send_own(desc_in, near_desc, desc_ssem, desc_rsem)
    for load in loads:
        load.wait()
    own = desc_ref[...].reshape(local * block, width)

    scaled = jnp.dot(own, wq_ref[...], preferred_element_type=jnp.float32) * (
        1.0 / math.sqrt(head_dim)
    )
    query[...] = scaled.astype(jnp.bfloat16).reshape(local, block, width)
    project(own, 1, blk)
    merged[...] = jnp.dot(
        own, wm_ref[pl.ds(0, width), :], preferred_element_type=jnp.float32
    ).reshape(merged.shape)
    wait_relayed(near_desc, desc_ssem, desc_rsem, 1, project_near)
    for section in (0, 2):
        relay(near_desc, desc_ssem, desc_rsem, section)
    for section in (0, 2):
        guarded(section - 1, lambda section=section: project_near(section, blk))
    for section in (0, 2):
        wait_relayed(near_desc, desc_ssem, desc_rsem, section, project_near)

    lanes = lax.broadcasted_iota(jnp.int32, (1, block), 1)
    rows_at = lax.broadcasted_iota(jnp.int32, (block, 1), 0)
    head_of = lax.broadcasted_iota(jnp.int32, (1, width), 1) // head_dim
    heads = [head_of == head for head in range(HEADS)]
    own_kpt = [kpt_ref[(img * blk_count + blk) * local + r] for r in range(local)]
    near_ids = [
        [jnp.clip(cov_ref[r, t] - first_block, 0, 3 * group - 1) for t in range(tiles)]
        for r in range(local)
    ]
    limits = [
        [
            jnp.where(t < count_ref[r], kpt_ref[jnp.clip(cov_ref[r, t], 0, kpt_ref.shape[0] - 1)], 0)
            for t in range(tiles)
        ]
        for r in range(local)
    ]
    biases = [
        [jnp.where(lanes < limits[r][t], 0.0, DEAD) for t in range(tiles)] for r in range(local)
    ]

    for r in range(local):
        keys = jnp.concatenate([near_k[near_ids[r][t]] for t in range(tiles)], axis=0)
        values = jnp.concatenate([near_v[near_ids[r][t]] for t in range(tiles)], axis=0)
        q = query[r]
        bias = jnp.concatenate(biases[r], axis=1)
        spans = [jnp.where(hit, q, jnp.zeros_like(q)) for hit in heads]
        stacked = lax.dot_general(
            jnp.concatenate(spans, axis=0),
            keys,
            (((1,), (1,)), ((), ())),
            preferred_element_type=jnp.float32,
        )
        message = jnp.zeros((block, width), jnp.float32)
        for head in range(HEADS):
            logits = stacked[head * block : (head + 1) * block] + bias
            weights = jnp.exp(logits - jnp.max(logits, axis=1, keepdims=True))
            inverse = 1.0 / jnp.sum(weights, axis=1, keepdims=True)
            out = jnp.dot(
                weights.astype(jnp.bfloat16), values, preferred_element_type=jnp.float32
            )
            message = jnp.where(heads[head], out * inverse, message)
        hidden = jnp.maximum(
            merged[r]
            + jnp.dot(
                message.astype(jnp.bfloat16),
                wm_ref[pl.ds(width, width), :],
                preferred_element_type=jnp.float32,
            ),
            0.0,
        ).astype(jnp.bfloat16)
        refined = desc_ref[r].astype(jnp.float32) + jnp.dot(
            hidden, wo_ref[...], preferred_element_type=jnp.float32
        )
        near_ref[group + blk * local + r] = refined.astype(jnp.bfloat16)

    own_slot = slot(near_ref, 1, blk)
    send_own(own_slot, near_ref, ref_ssem, ref_rsem)
    drain(desc_in, near_desc, desc_ssem, desc_rsem)
    for section in (0, 2):
        relay(near_ref, ref_ssem, ref_rsem, section)
    for section in (1, 0, 2):
        wait_relayed(near_ref, ref_ssem, ref_rsem, section)

    dust = dust_ref[0]
    row_live = [rows_at < own_kpt[r] for r in range(local)]
    for r in range(local):
        mine = near_ref[group + blk * local + r] * jnp.asarray(
            1.0 / math.sqrt(width), jnp.bfloat16
        )
        row_bias = jnp.where(row_live[r], 0.0, DEAD)
        for t in range(tiles):
            out = lax.dot_general(
                mine,
                near_ref[near_ids[r][t]],
                (((1,), (1,)), ((), ())),
                preferred_element_type=jnp.float32,
            )
            scores[r, t] = out + (row_bias + biases[r][t])

    slots = lax.broadcasted_iota(jnp.int32, (group, 1), 0)
    pots = [jnp.zeros((group, block), jnp.float32)] * 3

    def mass_copy(sweep, shift, member):
        first, count = max(0, shift), 3 - abs(shift)
        return pltpu.make_async_remote_copy(
            src_ref=acc.at[sweep, pl.ds(first, count)],
            dst_ref=mass_in.at[sweep, 2 - shift, blk, pl.ds(first, count)],
            send_sem=mass_ssem.at[sweep, shift + 2, member],
            recv_sem=mass_rsem.at[sweep, 2 - shift, blk],
            device_id=(img + shift, member),
            device_id_type=MESH,
        )

    def mass_arrival(sweep, source, member):
        first, count = max(0, -source), 3 - abs(source)
        here = mass_in.at[sweep, source + 2, member, pl.ds(first, count)]
        return pltpu.make_async_remote_copy(
            src_ref=here,
            dst_ref=here,
            send_sem=mass_ssem.at[sweep, source + 2, member],
            recv_sem=mass_rsem.at[sweep, source + 2, member],
            device_id=(img, others[0]),
            device_id_type=MESH,
        )

    def each_partner(body):
        for shift in (-1, 1, -2, 2, 0):
            def run(shift=shift):
                for member in others if shift == 0 else range(blk_count):
                    body(shift, member)
            guarded(shift, run)

    row_pots = [None] * local
    for sweep in range(ITERS):
        spread = [jnp.zeros((group, block), jnp.float32)] * 3
        for r in range(local):
            def shifted(t):
                if sweep == 0:
                    return scores[r, t]
                return scores[r, t] + pot[pl.ds(near_ids[r][t], 1), :]
            top = shifted(0)
            for t in range(1, tiles):
                top = jnp.maximum(top, shifted(t))
            top = jnp.maximum(jnp.max(top, axis=1, keepdims=True), dust)
            terms = [jnp.exp(shifted(t) - top) for t in range(tiles)]
            total = functools.reduce(jnp.add, terms)
            total = jnp.sum(total, axis=1, keepdims=True) + jnp.exp(dust - top)
            row_pots[r] = -(top + jnp.log(total))
            inverse = 1.0 / total
            for t in range(tiles):
                mass = jnp.sum(terms[t] * inverse, axis=0, keepdims=True)
                for section in range(3):
                    hit = slots == near_ids[r][t] - section * group
                    spread[section] = spread[section] + jnp.where(hit, mass, 0.0)
        for section in range(3):
            acc[sweep, section] = spread[section]
        each_partner(lambda shift, member: mass_copy(sweep, shift, member).start())
        if sweep == 0:
            drain(own_slot, near_ref, ref_ssem, ref_rsem)
        if sweep == ITERS - 1:
            for r in range(local):
                row = jnp.broadcast_to(row_pots[r], (block, block))
                row = jnp.sum(jnp.where(rows_at == lanes, row, 0.0), axis=0, keepdims=True)
                tail_ref[pl.ds(local * tiles + r, 1), :] = jnp.where(lanes < own_kpt[r], dust + row, 0.0)
                for t in range(tiles):
                    scores[r, t] = scores[r, t] + row_pots[r]
        sums = list(spread)
        each_partner(lambda source, member: mass_arrival(sweep, source, member).wait_recv())
        for source in range(-2, 3):
            for member in others if source == 0 else range(blk_count):
                for section in range(3):
                    if 0 <= section - source <= 2:
                        sums[section] = sums[section] + mass_in[
                            sweep, source + 2, member, section - source
                        ]
        for section in range(3):
            pots[section] = pots[section] - jnp.log(
                sums[section] + jnp.exp(dust + pots[section])
            )
            pot[pl.ds(section * group, group), :] = pots[section]

    for r in range(local):
        for t in range(tiles):
            tail_ref[pl.ds(r * tiles + t, 1), :] = pot[pl.ds(near_ids[r][t], 1), :]
        mine = pot[pl.ds(group + blk * local + r, 1), :]
        tail_ref[pl.ds(local * (tiles + 1) + r, 1), :] = jnp.where(lanes < own_kpt[r], dust + mine, 0.0)
    for sweep in range(ITERS):
        each_partner(lambda shift, member: mass_copy(sweep, shift, member).wait_send())


def finish(base_ref, tail_ref, plan_out, row_out, col_out, made, out_sem, end_sem):
    local, tiles = base_ref.shape[:2]
    places = [(r, t) for r in range(local) for t in range(tiles)]

    def put(r, t):
        return pltpu.make_async_copy(made.at[r, t], plan_out.at[r, t], out_sem.at[r, t])

    ends = [
        pltpu.make_async_copy(
            tail_ref.at[pl.ds(local * (tiles + step), local)], target, end_sem.at[step]
        )
        for step, target in enumerate((row_out, col_out))
    ]
    for end in ends:
        end.start()
    for r, t in places:
        base = base_ref[r, t]
        out = base + tail_ref[pl.ds(r * tiles + t, 1), :]
        made[r, t] = jnp.where(base > 0.1 * DEAD, out, 0.0)
        put(r, t).start()
    for place in places:
        put(*place).wait()
    for end in ends:
        end.wait()


def on_device(
    img_count,
    blk_count,
    descriptors,
    covisible,
    tile_counts,
    keypoints,
    query_weight,
    key_weight,
    value_weight,
    merge_weight,
    output_weight,
    dustbin,
):
    local, block, width = descriptors.shape
    tiles = covisible.shape[1]
    group = local * blk_count
    near = 3 * group
    vmem = pl.BlockSpec(memory_space=pltpu.VMEM)
    hbm = pl.BlockSpec(memory_space=pltpu.HBM)
    dma = pltpu.SemaphoreType.DMA
    half = jnp.bfloat16
    full = jnp.float32
    base, tail = pl.pallas_call(
        functools.partial(kernel, img_count, blk_count),
        out_shape=(
            pltpu.VMEM((local, tiles, block, block), full),
            pltpu.VMEM((local * (tiles + 2), block), full),
        ),
        in_specs=[hbm] * 10,
        out_specs=(vmem, vmem),
        scratch_shapes=[
            pltpu.VMEM(descriptors.shape, half),
            pltpu.SMEM(covisible.shape, jnp.int32),
            pltpu.SMEM(tile_counts.shape, jnp.int32),
            pltpu.SMEM(keypoints.shape, jnp.int32),
            pltpu.VMEM(query_weight.shape, half),
            pltpu.VMEM(key_weight.shape, half),
            pltpu.VMEM(value_weight.shape, half),
            pltpu.VMEM(merge_weight.shape, half),
            pltpu.VMEM(output_weight.shape, half),
            pltpu.SMEM(dustbin.shape, full),
            dma((10,)),
            pltpu.VMEM((near, block, width), half),
            pltpu.VMEM((near, block, width), half),
            pltpu.VMEM((near, block, width), half),
            pltpu.VMEM((near, block, width), half),
            pltpu.VMEM((local, block, width), half),
            pltpu.VMEM((local, block, merge_weight.shape[1]), full),
            pltpu.VMEM((ITERS, 3, group, block), full),
            pltpu.VMEM((ITERS, 5, blk_count, 3, group, block), full),
            pltpu.VMEM((near, block), full),
            dma((3, blk_count)),
            dma((3, blk_count)),
            dma((3, blk_count)),
            dma((3, blk_count)),
            dma((ITERS, 5, blk_count)),
            dma((ITERS, 5, blk_count)),
        ],
        compiler_params=pltpu.CompilerParams(
            collective_id=0, has_side_effects=True, vmem_limit_bytes=VMEM_BYTES
        ),
    )(
        *(
            pltpu.with_memory_space_constraint(x, pltpu.HBM)
            for x in (
                descriptors,
                covisible,
                tile_counts,
                keypoints,
                query_weight,
                key_weight,
                value_weight,
                merge_weight,
                output_weight,
            )
        ),
        dustbin,
    )
    return pl.pallas_call(
        finish,
        out_shape=(
            jax.ShapeDtypeStruct(base.shape, full),
            jax.ShapeDtypeStruct((local, block), full),
            jax.ShapeDtypeStruct((local, block), full),
        ),
        in_specs=[vmem, vmem],
        out_specs=(hbm, hbm, hbm),
        scratch_shapes=[
            pltpu.VMEM(base.shape, full),
            dma((local, tiles)),
            dma((2,)),
        ],
        compiler_params=pltpu.CompilerParams(vmem_limit_bytes=VMEM_BYTES),
    )(*(pltpu.with_memory_space_constraint(x, pltpu.VMEM) for x in (base, tail)))


def solution(mesh):
    in_specs = (
        P(("img", "blk"), None, None),
        P(("img", "blk"), None),
        P(("img", "blk")),
        P(),
        P(),
        P(),
        P(),
        P(),
        P(),
        P(),
    )
    out_specs = (
        P(("img", "blk"), None, None, None),
        P(("img", "blk"), None),
        P(("img", "blk"), None),
    )
    return jax.shard_map(
        functools.partial(on_device, mesh.shape["img"], mesh.shape["blk"]),
        mesh=mesh,
        in_specs=in_specs,
        out_specs=out_specs,
        check_vma=False,
    )
```

```python
import functools
import math

import jax
import jax.numpy as jnp
from jax import lax
from jax.experimental import pallas as pl
from jax.experimental.pallas import tpu as pltpu
from jax.sharding import PartitionSpec as P

HEADS = 4
ITERS = 3
DEAD = -1e30
MESH = pl.DeviceIdType.MESH
VMEM_BYTES = 48 * 1024 * 1024


def kernel(
    img_count,
    blk_count,
    desc_in,
    cov_in,
    count_in,
    kpt_in,
    wq_in,
    wk_in,
    wv_in,
    wm_in,
    wo_in,
    dust_in,
    scores,
    tail_ref,
    desc_ref,
    cov_ref,
    count_ref,
    kpt_ref,
    dust_ref,
    weights_ref,
    load_sem,
    near_desc,
    near_ref,
    value_turned,
    spans,
    merged,
    slot_limit,
    top_ref,
    sum_ref,
    mix_ref,
    logit_ref,
    dots,
    acc,
    mass_in,
    pot,
    send_sem,
    pair_sem,
    direct_sem,
    passed_sem,
    mass_ssem,
    mass_rsem,
):
    local, block, width = desc_ref.shape
    tiles = cov_ref.shape[1]
    group = local * blk_count
    head_dim = width // HEADS
    deep = wm_in.shape[1]
    img = lax.axis_index("img")
    blk = lax.axis_index("blk")
    others = [lax.rem(blk + step, blk_count) for step in range(1, blk_count)]
    first_block = (img - 1) * group
    far = 2 * lax.rem(img, 2) - 1
    near = -far

    def exists(shift):
        if isinstance(shift, int):
            return img + shift < img_count if shift > 0 else img + shift >= 0
        return jnp.logical_and(img + shift >= 0, img + shift < img_count)

    has_far, has_near = exists(far), exists(near)

    sizes = (width, width, width, deep)
    starts = [sum(sizes[:place]) for place in range(len(sizes) + 1)]
    weight_rows = [(wq_in, 0), (wk_in, 0), (wv_in, 0), (wo_in, 0)]
    weight_rows += [(wm_in, column) for column in range(0, deep, width)]
    loads = []
    start = 0
    for source, column in weight_rows:
        count = source.shape[0]
        loads.append(
            pltpu.make_async_copy(
                source.at[:, pl.ds(column, width)],
                weights_ref.at[pl.ds(start, count)],
                load_sem.at[0],
            )
        )
        start += count
    weight_load = pltpu.make_async_copy(weights_ref, weights_ref, load_sem.at[0])
    small_loads = [
        pltpu.make_async_copy(source, target, load_sem.at[1 + place])
        for place, (source, target) in enumerate(
            (
                (desc_in, desc_ref),
                (cov_in, cov_ref),
                (count_in, count_ref),
                (kpt_in, kpt_ref),
                (dust_in, dust_ref),
            )
        )
    ]

    def weight(place):
        return weights_ref[pl.ds(starts[place], sizes[place]), :]

    def merge_part(step, column):
        first = starts[4] + column * 2 * width + step * width
        return weights_ref[pl.ds(first, width), :]

    barrier = pltpu.get_barrier_semaphore()

    def greet(shift, member):
        pl.semaphore_signal(
            barrier, inc=1, device_id=(img + shift, member), device_id_type=MESH
        )

    for shift in (far, near):
        pl.when(exists(shift))(lambda shift=shift: greet(shift, blk))
    for member in others:
        greet(0, member)

    for load in small_loads + loads:
        load.start()

    def slot_of(section, member, place):
        return (section * blk_count + member) * local + place

    def push(phase, source, slot, rsem, device):
        room = (near_desc, near_ref)[phase]
        pltpu.make_async_remote_copy(
            src_ref=source,
            dst_ref=room.at[slot],
            send_sem=send_sem.at[phase],
            recv_sem=rsem,
            device_id=device,
            device_id_type=MESH,
        ).start()

    def received(phase, rsem, first, count):
        room = (near_desc, near_ref)[phase]
        here = room.at[pl.ds(first, count)]
        pltpu.make_async_remote_copy(
            src_ref=here,
            dst_ref=here,
            send_sem=send_sem.at[phase],
            recv_sem=rsem,
            device_id=(img, others[0]),
            device_id_type=MESH,
        ).wait_recv()

    sides = ((has_far, far), (has_near, near))

    def send_own(phase, source):
        for place in range(local):
            for member in others:
                push(
                    phase,
                    source(place),
                    slot_of(1, blk, place),
                    pair_sem.at[phase],
                    (img, member),
                )
        for order, (there, shift) in enumerate(sides):
            @pl.when(there)
            def _(order=order, shift=shift):
                for place in range(local):
                    push(
                        phase,
                        source(place),
                        slot_of(1 - shift, blk, place),
                        direct_sem.at[phase, order, place],
                        (img + shift, blk),
                    )

    def collect(phase, use):
        room = (near_desc, near_ref)[phase]
        count = len(others)

        def relay(order, place):
            slot = slot_of(1 + sides[order][1], blk, place)
            received(phase, direct_sem.at[phase, order, place], slot, 1)
            for member in others:
                push(
                    phase, room.at[slot], slot, passed_sem.at[phase, order, place], (img, member)
                )

        def piece(order, place):
            section = 1 + sides[order][1]
            first = slot_of(section, others[0], place) if count == 1 else 0
            received(phase, passed_sem.at[phase, order, place], first, count)
            use([slot_of(section, member, place) for member in range(blk_count)])

        first = slot_of(1, others[0], 0) if count == 1 else 0
        received(phase, pair_sem.at[phase], first, count * local)
        use([slot_of(1, member, place) for member in others for place in range(local)])

        @pl.when(has_far)
        def _():
            for place in range(local):
                relay(0, place)
            for place in range(local - 1):
                piece(0, place)

        @pl.when(has_near)
        def _():
            for place in range(local - 1):
                relay(1, place)

        @pl.when(has_far)
        def _():
            piece(0, local - 1)

        @pl.when(has_near)
        def _():
            relay(1, local - 1)
            for place in range(local):
                piece(1, place)

    def drain(phase):
        for with_far in (False, True):
            for with_near in (False, True):
                count = local * len(others)
                count += (with_far + with_near) * local * (1 + len(others))

                @pl.when(jnp.logical_and(has_far == with_far, has_near == with_near))
                def _(count=count):
                    here = near_ref.at[pl.ds(0, count)]
                    pltpu.make_async_remote_copy(
                        src_ref=here,
                        dst_ref=here,
                        send_sem=send_sem.at[phase],
                        recv_sem=send_sem.at[phase],
                        device_id=(img, others[0]),
                        device_id_type=MESH,
                    ).wait_send()

    def mass_at(source, member):
        count = 3 - abs(source)
        base = {0: 0, -1: 3, 1: 5, -2: 7, 2: 8}[source] * blk_count
        return base + member * count, count

    for source in range(-2, 3):
        if source != 0:
            @pl.when(jnp.logical_not(exists(source)))
            def _(source=source):
                first = mass_at(source, 0)[0]
                count = mass_at(source, blk_count)[0] - first
                for sweep in range(ITERS):
                    mass_in[sweep, pl.ds(first, count)] = jnp.zeros(
                        (count, group, block), jnp.float32
                    )
    for source in (-1, 1):
        @pl.when(jnp.logical_not(exists(source)))
        def _(source=source):
            for r in range(local):
                for spot in range(group):
                    dots[r, (1 + source) * group + spot] = jnp.zeros((block, block), jnp.float32)

    pl.semaphore_wait(
        barrier, len(others) + has_far.astype(jnp.int32) + has_near.astype(jnp.int32)
    )
    send_own(0, lambda place: desc_in.at[place])
    for load in small_loads:
        load.wait()
    weight_load.wait()

    lanes = lax.broadcasted_iota(jnp.int32, (1, block), 1)
    rows_at = lax.broadcasted_iota(jnp.int32, (block, 1), 0)
    head_of = lax.broadcasted_iota(jnp.int32, (1, width), 1) // head_dim
    own_kpt = [kpt_ref[(img * blk_count + blk) * local + r] for r in range(local)]
    near_ids = [
        [jnp.clip(cov_ref[r, t] - first_block, 0, 3 * group - 1) for t in range(tiles)]
        for r in range(local)
    ]
    limits = [
        [
            jnp.where(t < count_ref[r], kpt_ref[jnp.clip(cov_ref[r, t], 0, kpt_ref.shape[0] - 1)], 0)
            for t in range(tiles)
        ]
        for r in range(local)
    ]
    biases = [
        [jnp.where(lanes < limits[r][t], 0.0, DEAD) for t in range(tiles)] for r in range(local)
    ]
    for r in range(local):
        for spot in range(3 * group):
            limit = 0
            for t in range(tiles):
                limit = jnp.where(near_ids[r][t] == spot, limits[r][t], limit)
            slot_limit[r, spot] = limit

    own = desc_ref[...].reshape(local * block, width)
    query = jnp.dot(own, weight(0), preferred_element_type=jnp.float32).astype(jnp.bfloat16)
    for r in range(local):
        q = query[r * block : (r + 1) * block]
        turned = lax.dot_general(
            jnp.concatenate(
                [jnp.where(head_of == head, q, jnp.zeros_like(q)) for head in range(HEADS)], axis=0
            ),
            weight(1),
            (((1,), (1,)), ((), ())),
            preferred_element_type=jnp.float32,
        )
        spans[r] = (turned * (math.log2(math.e) / math.sqrt(head_dim))).astype(jnp.bfloat16)
    value_turned[...] = weight(2).T
    columns = deep // width
    for column in range(columns):
        merged[:, pl.ds(column * width, width)] = jnp.dot(
            own, merge_part(0, column), preferred_element_type=jnp.float32
        )
    places_at = lax.broadcasted_iota(jnp.int32, (block, block), 0)
    step_heads = 2 if HEADS % 2 == 0 else 1

    def attend(rows, spots, first=False):
        values = lax.dot_general(
            value_turned[...], rows, (((1,), (1,)), ((), ())), preferred_element_type=jnp.float32
        ).astype(jnp.bfloat16)
        lives = [[places_at < slot_limit[r, spot] for spot in spots] for r in range(local)]
        chains = [(r, base) for r in range(local) for base in range(0, HEADS, step_heads)]

        def compare(chain):
            r, base = chain
            logits = lax.dot_general(
                rows,
                spans[r, pl.ds(base * block, step_heads * block)],
                (((1,), (1,)), ((), ())),
                preferred_element_type=jnp.float32,
            )
            tops = []
            for head in range(step_heads):
                top = None
                for place, alive in enumerate(lives[r]):
                    where_to = (pl.ds(place * block, block), pl.ds(head * block, block))
                    part = jnp.where(
                        alive,
                        logits[
                            place * block : (place + 1) * block,
                            head * block : (head + 1) * block,
                        ],
                        DEAD,
                    )
                    logit_ref[r, base // step_heads, where_to[0], where_to[1]] = part
                    top = part if top is None else jnp.maximum(top, part)
                tops.append(jnp.max(top, axis=0, keepdims=True))
            return tops

        def soften(chain, logits):
            r, base = chain
            weights = []
            scales = []
            for head in range(step_heads):
                where_to = pl.ds(base + head, 1)
                parts = [
                    logit_ref[
                        r,
                        base // step_heads,
                        pl.ds(place * block, block),
                        pl.ds(head * block, block),
                    ]
                    for place in range(len(spots))
                ]
                top = logits[head]
                if not first:
                    old = top_ref[r, where_to, :]
                    top = jnp.maximum(top, old)
                    scales.append(jnp.exp2(old - top))
                parts = [jnp.exp2(part - top) for part in parts]
                total = jnp.sum(functools.reduce(jnp.add, parts), axis=0, keepdims=True)
                if not first:
                    total = total + sum_ref[r, where_to, :] * scales[head]
                top_ref[r, where_to, :] = top
                sum_ref[r, where_to, :] = total
                weights.append(
                    jnp.concatenate([part.astype(jnp.bfloat16) for part in parts], axis=0)
                )
            return jnp.concatenate(weights, axis=1), scales

        def blend(chain, weights, scales):
            r, base = chain
            out = jnp.dot(
                values[base * head_dim : (base + step_heads) * head_dim],
                weights,
                preferred_element_type=jnp.float32,
            )
            for head in range(step_heads):
                where_to = pl.ds((base + head) * head_dim, head_dim)
                mix = out[
                    head * head_dim : (head + 1) * head_dim, head * block : (head + 1) * block
                ]
                if not first:
                    mix = mix + mix_ref[r, where_to, :] * scales[head]
                mix_ref[r, where_to, :] = mix

        compared = [compare(chain) for chain in chains]
        softened = [soften(chain, logits) for chain, logits in zip(chains, compared)]
        for chain, soft in zip(chains, softened):
            blend(chain, *soft)

    def attend_near(spots):
        attend(jnp.concatenate([near_desc[spot] for spot in spots], axis=0), spots)

    attend(own, [slot_of(1, blk, place) for place in range(local)], first=True)
    collect(0, attend_near)

    message = jnp.concatenate(
        [
            jnp.concatenate(
                [
                    mix_ref[r, pl.ds(head * head_dim, head_dim), :]
                    * (1.0 / sum_ref[r, pl.ds(head, 1), :])
                    for head in range(HEADS)
                ],
                axis=0,
            )
            for r in range(local)
        ],
        axis=1,
    ).astype(jnp.bfloat16)
    refined = desc_ref[...].reshape(local * block, width).astype(jnp.float32)
    for column in range(columns):
        hidden = jnp.maximum(
            merged[:, pl.ds(column * width, width)]
            + lax.dot_general(
                message,
                merge_part(1, column),
                (((0,), (0,)), ((), ())),
                preferred_element_type=jnp.float32,
            ),
            0.0,
        ).astype(jnp.bfloat16)
        refined = refined + jnp.dot(
            hidden,
            weights_ref[pl.ds(starts[3] + column * width, width), :],
            preferred_element_type=jnp.float32,
        )
    refined = refined.astype(jnp.bfloat16)
    near_ref[pl.ds(slot_of(1, blk, 0), local)] = refined.reshape(local, block, width)
    send_own(1, lambda place: near_ref.at[slot_of(1, blk, place)])

    mine = refined * jnp.asarray(1.0 / math.sqrt(width), jnp.bfloat16)

    def multiply(spots):
        theirs = jnp.concatenate([near_ref[spot] for spot in spots], axis=0)
        out = lax.dot_general(
            mine, theirs, (((1,), (1,)), ((), ())), preferred_element_type=jnp.float32
        )
        for r in range(local):
            for place, spot in enumerate(spots):
                dots[r, spot] = out[
                    r * block : (r + 1) * block, place * block : (place + 1) * block
                ]

    multiply([slot_of(1, blk, place) for place in range(local)])
    collect(1, multiply)

    dust = dust_ref[0]
    row_live = [rows_at < own_kpt[r] for r in range(local)]
    row_bias = [jnp.where(row_live[r], 0.0, DEAD) for r in range(local)]

    slots = lax.broadcasted_iota(jnp.int32, (group, 1), 0)
    pots = [jnp.zeros((group, block), jnp.float32)] * 3

    def mass_start(sweep, shift, member):
        first, count = mass_at(-shift, blk)
        pltpu.make_async_remote_copy(
            src_ref=acc.at[sweep, pl.ds(max(0, shift), count)],
            dst_ref=mass_in.at[sweep, pl.ds(first, count)],
            send_sem=mass_ssem.at[sweep],
            recv_sem=mass_rsem.at[sweep],
            device_id=(img + shift, member),
            device_id_type=MESH,
        ).start()

    def mass_wait(sweep, wait):
        for below in range(3):
            for above in range(3):
                count = 3 * len(others)
                for reach in (below, above):
                    count += sum((3 - step) * blk_count for step in range(1, reach + 1))

                @pl.when(
                    jnp.logical_and(
                        jnp.minimum(img, 2) == below,
                        jnp.minimum(img_count - 1 - img, 2) == above,
                    )
                )
                def _(count=count):
                    here = mass_in.at[sweep, pl.ds(0, count)]
                    wait(
                        pltpu.make_async_remote_copy(
                            src_ref=here,
                            dst_ref=here,
                            send_sem=mass_ssem.at[sweep],
                            recv_sem=mass_rsem.at[sweep],
                            device_id=(img, others[0]),
                            device_id_type=MESH,
                        )
                    )

    def each_partner(body):
        for shift in (-1, 1, -2, 2):
            def run(shift=shift):
                for member in range(blk_count):
                    body(shift, member)
            pl.when(exists(shift))(run)
        for member in others:
            body(0, member)

    row_pots = [None] * local
    for sweep in range(ITERS):
        spread = [jnp.zeros((group, block), jnp.float32)] * 3
        for r in range(local):
            if sweep == 0:
                for t in range(tiles):
                    scores[r, t] = dots[r, near_ids[r][t]] + (row_bias[r] + biases[r][t])

            def shifted(t):
                if sweep == 0:
                    return scores[r, t]
                return scores[r, t] + pot[pl.ds(near_ids[r][t], 1), :]
            top = shifted(0)
            for t in range(1, tiles):
                top = jnp.maximum(top, shifted(t))
            top = jnp.maximum(jnp.max(top, axis=1, keepdims=True), dust)
            terms = [jnp.exp(shifted(t) - top) for t in range(tiles)]
            total = functools.reduce(jnp.add, terms)
            total = jnp.sum(total, axis=1, keepdims=True) + jnp.exp(dust - top)
            row_pots[r] = -(top + jnp.log(total))
            inverse = 1.0 / total
            for t in range(tiles):
                mass = jnp.sum(terms[t] * inverse, axis=0, keepdims=True)
                for section in range(3):
                    hit = slots == near_ids[r][t] - section * group
                    spread[section] = spread[section] + jnp.where(hit, mass, 0.0)
        for section in range(3):
            acc[sweep, section] = spread[section]
        each_partner(lambda shift, member: mass_start(sweep, shift, member))
        if sweep == 0:
            drain(0)
            drain(1)
        if sweep == ITERS - 1:
            for r in range(local):
                row = jnp.broadcast_to(row_pots[r], (block, block))
                row = jnp.sum(jnp.where(rows_at == lanes, row, 0.0), axis=0, keepdims=True)
                tail_ref[pl.ds(local * tiles + r, 1), :] = jnp.where(lanes < own_kpt[r], dust + row, 0.0)
                for t in range(tiles):
                    scores[r, t] = scores[r, t] + row_pots[r]
        sums = list(spread)
        mass_wait(sweep, lambda copy: copy.wait_recv())
        for source in range(-2, 3):
            for member in others if source == 0 else range(blk_count):
                for section in range(max(0, source), 3 + min(0, source)):
                    first, _ = mass_at(source, member)
                    sums[section] = sums[section] + mass_in[
                        sweep, first + section - max(0, source)
                    ]
        for section in range(3):
            pots[section] = pots[section] - jnp.log(
                sums[section] + jnp.exp(dust + pots[section])
            )
            pot[pl.ds(section * group, group), :] = pots[section]

    for r in range(local):
        for t in range(tiles):
            tail_ref[pl.ds(r * tiles + t, 1), :] = pot[pl.ds(near_ids[r][t], 1), :]
        mine = pot[pl.ds(group + blk * local + r, 1), :]
        tail_ref[pl.ds(local * (tiles + 1) + r, 1), :] = jnp.where(lanes < own_kpt[r], dust + mine, 0.0)
    for sweep in range(ITERS):
        mass_wait(sweep, lambda copy: copy.wait_send())


def finish(base_ref, tail_ref, plan_out, row_out, col_out, made, out_sem, end_sem):
    local, tiles = base_ref.shape[:2]
    places = [(r, t) for r in range(local) for t in range(tiles)]

    def put(r, t):
        return pltpu.make_async_copy(made.at[r, t], plan_out.at[r, t], out_sem)

    ends = [
        pltpu.make_async_copy(
            tail_ref.at[pl.ds(local * (tiles + step), local)], target, end_sem.at[step]
        )
        for step, target in enumerate((row_out, col_out))
    ]
    for end in ends:
        end.start()
    for r, t in places:
        base = base_ref[r, t]
        out = base + tail_ref[pl.ds(r * tiles + t, 1), :]
        made[r, t] = jnp.where(base > 0.1 * DEAD, out, 0.0)
        put(r, t).start()
    for end in ends:
        end.wait()
    pltpu.make_async_copy(made, plan_out, out_sem).wait()


def on_device(
    img_count,
    blk_count,
    descriptors,
    covisible,
    tile_counts,
    keypoints,
    query_weight,
    key_weight,
    value_weight,
    merge_weight,
    output_weight,
    dustbin,
):
    local, block, width = descriptors.shape
    tiles = covisible.shape[1]
    group = local * blk_count
    near = 3 * group
    most = max(local * (blk_count - 1), blk_count, local)
    pace = 2 if HEADS % 2 == 0 else 1
    weight_rows = (
        3 * width
        + output_weight.shape[0]
        + merge_weight.shape[0] * (merge_weight.shape[1] // width)
    )
    vmem = pl.BlockSpec(memory_space=pltpu.VMEM)
    hbm = pl.BlockSpec(memory_space=pltpu.HBM)
    dma = pltpu.SemaphoreType.DMA
    half = jnp.bfloat16
    full = jnp.float32
    base, tail = pl.pallas_call(
        functools.partial(kernel, img_count, blk_count),
        out_shape=(
            pltpu.VMEM((local, tiles, block, block), full),
            pltpu.VMEM((local * (tiles + 2), block), full),
        ),
        in_specs=[hbm] * 10,
        out_specs=(vmem, vmem),
        scratch_shapes=[
            pltpu.VMEM(descriptors.shape, half),
            pltpu.SMEM(covisible.shape, jnp.int32),
            pltpu.SMEM(tile_counts.shape, jnp.int32),
            pltpu.SMEM(keypoints.shape, jnp.int32),
            pltpu.SMEM(dustbin.shape, full),
            pltpu.VMEM((weight_rows, width), half),
            dma((6,)),
            pltpu.VMEM((near, block, width), half),
            pltpu.VMEM((near, block, width), half),
            pltpu.VMEM(value_weight.shape, half),
            pltpu.VMEM((local, HEADS * block, width), half),
            pltpu.VMEM((local * block, merge_weight.shape[1]), full),
            pltpu.SMEM((local, near), jnp.int32),
            pltpu.VMEM((local, HEADS, block), full),
            pltpu.VMEM((local, HEADS, block), full),
            pltpu.VMEM((local, width, block), full),
            pltpu.VMEM((local, HEADS // pace, most * block, pace * block), full),
            pltpu.VMEM((local, near, block, block), full),
            pltpu.VMEM((ITERS, 3, group, block), full),
            pltpu.VMEM((ITERS, 9 * blk_count, group, block), full),
            pltpu.VMEM((near, block), full),
            dma((2,)),
            dma((2,)),
            dma((2, 2, local)),
            dma((2, 2, local)),
            dma((ITERS,)),
            dma((ITERS,)),
        ],
        compiler_params=pltpu.CompilerParams(
            collective_id=0, has_side_effects=True, vmem_limit_bytes=VMEM_BYTES
        ),
    )(
        *(
            pltpu.with_memory_space_constraint(x, pltpu.HBM)
            for x in (
                descriptors,
                covisible,
                tile_counts,
                keypoints,
                query_weight,
                key_weight,
                value_weight,
                merge_weight,
                output_weight,
            )
        ),
        dustbin,
    )
    return pl.pallas_call(
        finish,
        out_shape=(
            jax.ShapeDtypeStruct(base.shape, full),
            jax.ShapeDtypeStruct((local, block), full),
            jax.ShapeDtypeStruct((local, block), full),
        ),
        in_specs=[vmem, vmem],
        out_specs=(hbm, hbm, hbm),
        scratch_shapes=[
            pltpu.VMEM(base.shape, full),
            dma,
            dma((2,)),
        ],
        compiler_params=pltpu.CompilerParams(vmem_limit_bytes=VMEM_BYTES),
    )(*(pltpu.with_memory_space_constraint(x, pltpu.VMEM) for x in (base, tail)))


def solution(mesh):
    in_specs = (
        P(("img", "blk"), None, None),
        P(("img", "blk"), None),
        P(("img", "blk")),
        P(),
        P(),
        P(),
        P(),
        P(),
        P(),
        P(),
    )
    out_specs = (
        P(("img", "blk"), None, None, None),
        P(("img", "blk"), None),
        P(("img", "blk"), None),
    )
    return jax.shard_map(
        functools.partial(on_device, mesh.shape["img"], mesh.shape["blk"]),
        mesh=mesh,
        in_specs=in_specs,
        out_specs=out_specs,
        check_vma=False,
    )
```

```python
import functools
import math

import jax
import jax.numpy as jnp
from jax import lax
from jax.experimental import pallas as pl
from jax.experimental.pallas import tpu as pltpu
from jax.sharding import PartitionSpec as P

HEADS = 4
ITERS = 3
DEAD = -1e30
LOG2E = math.log2(math.e)
LN2 = math.log(2.0)
MESH = pl.DeviceIdType.MESH
VMEM_BYTES = 48 * 1024 * 1024


def kernel(
    img_count,
    blk_count,
    desc_in,
    cov_in,
    count_in,
    kpt_in,
    wq_in,
    wk_in,
    wv_in,
    wm_in,
    wo_in,
    dust_in,
    scores,
    tail_ref,
    desc_ref,
    cov_ref,
    count_ref,
    kpt_ref,
    dust_ref,
    weights_ref,
    load_sem,
    near_desc,
    near_ref,
    value_turned,
    spans,
    merged,
    slot_limit,
    top_ref,
    sum_ref,
    mix_ref,
    logit_ref,
    dots,
    shifted,
    acc,
    mass_in,
    pot,
    send_sem,
    pair_sem,
    direct_sem,
    passed_sem,
    mass_ssem,
    mass_rsem,
):
    local, block, width = desc_ref.shape
    tiles = cov_ref.shape[1]
    group = local * blk_count
    head_dim = width // HEADS
    deep = wm_in.shape[1]
    img = lax.axis_index("img")
    blk = lax.axis_index("blk")
    others = [lax.rem(blk + step, blk_count) for step in range(1, blk_count)]
    first_block = (img - 1) * group
    far = 2 * lax.rem(img, 2) - 1
    near = -far

    def exists(shift):
        if isinstance(shift, int):
            return img + shift < img_count if shift > 0 else img + shift >= 0
        return jnp.logical_and(img + shift >= 0, img + shift < img_count)

    has_far = exists(far)
    has_near = True if img_count % 2 == 0 else exists(near)

    def when(condition):
        return (lambda body: body()) if condition is True else pl.when(condition)


    sizes = (width, width, width, deep)
    starts = [sum(sizes[:place]) for place in range(len(sizes) + 1)]
    weight_rows = [(wq_in, 0), (wk_in, 0), (wv_in, 0), (wo_in, 0)]
    weight_rows += [(wm_in, column) for column in range(0, deep, width)]
    loads = []
    start = 0
    for source, column in weight_rows:
        count = source.shape[0]
        loads.append(
            pltpu.make_async_copy(
                source.at[:, pl.ds(column, width)],
                weights_ref.at[pl.ds(start, count)],
                load_sem.at[0],
            )
        )
        start += count
    weight_load = pltpu.make_async_copy(weights_ref, weights_ref, load_sem.at[0])
    small_loads = [
        pltpu.make_async_copy(source, target, load_sem.at[1 + place])
        for place, (source, target) in enumerate(
            (
                (desc_in, desc_ref),
                (cov_in, cov_ref),
                (count_in, count_ref),
                (kpt_in, kpt_ref),
                (dust_in, dust_ref),
            )
        )
    ]

    def weight(place):
        return weights_ref[pl.ds(starts[place], sizes[place]), :]

    def merge_part(step, column):
        first = starts[4] + column * 2 * width + step * width
        return weights_ref[pl.ds(first, width), :]

    barrier = pltpu.get_barrier_semaphore()

    def greet(shift, member):
        pl.semaphore_signal(
            barrier, inc=1, device_id=(img + shift, member), device_id_type=MESH
        )

    when(has_far)(lambda: greet(far, blk))
    when(has_near)(lambda: greet(near, blk))
    for member in others:
        greet(0, member)

    for load in small_loads + loads:
        load.start()

    def slot_of(section, member, place):
        return (section * blk_count + member) * local + place

    def push(phase, source, slot, rsem, device):
        room = (near_desc, near_ref)[phase]
        pltpu.make_async_remote_copy(
            src_ref=source,
            dst_ref=room.at[slot],
            send_sem=send_sem.at[phase],
            recv_sem=rsem,
            device_id=device,
            device_id_type=MESH,
        ).start()

    def received(phase, rsem, first, count):
        room = (near_desc, near_ref)[phase]
        here = room.at[pl.ds(first, count)]
        pltpu.make_async_remote_copy(
            src_ref=here,
            dst_ref=here,
            send_sem=send_sem.at[phase],
            recv_sem=rsem,
            device_id=(img, others[0]),
            device_id_type=MESH,
        ).wait_recv()

    sides = ((has_far, far), (has_near, near))

    def send_own(phase, source):
        for place in range(local):
            for member in others:
                push(
                    phase,
                    source(place),
                    slot_of(1, blk, place),
                    pair_sem.at[phase],
                    (img, member),
                )
        for order, (there, shift) in enumerate(sides):
            @when(there)
            def _(order=order, shift=shift):
                for place in range(local):
                    push(
                        phase,
                        source(place),
                        slot_of(1 - shift, blk, place),
                        direct_sem.at[phase, order, place],
                        (img + shift, blk),
                    )

    def collect(phase, use):
        room = (near_desc, near_ref)[phase]
        count = len(others)

        def relay(order, place):
            slot = slot_of(1 + sides[order][1], blk, place)
            received(phase, direct_sem.at[phase, order, place], slot, 1)
            for member in others:
                push(
                    phase, room.at[slot], slot, passed_sem.at[phase, order, place], (img, member)
                )

        def passed(order, place):
            section = 1 + sides[order][1]
            first = slot_of(section, others[0], place) if count == 1 else 0
            received(phase, passed_sem.at[phase, order, place], first, count)
            return [slot_of(section, member, place) for member in range(blk_count)]

        def piece(order, place):
            use(passed(order, place))

        first = slot_of(1, others[0], 0) if count == 1 else 0
        received(phase, pair_sem.at[phase], first, count * local)
        use([slot_of(1, member, place) for member in others for place in range(local)])

        @pl.when(has_far)
        def _():
            for place in range(local):
                relay(0, place)
            for place in range(local - 1):
                piece(0, place)

        @when(has_near)
        def _():
            for place in range(local - 1):
                relay(1, place)

        @pl.when(has_far)
        def _():
            piece(0, local - 1)

        @when(has_near)
        def _():
            last = local - 1
            relay(1, last)
            spots = [slot_of(1 + near, blk, last)]
            for place in range(last):
                spots += passed(1, place)
            use(spots)
            passed(1, last)
            use([slot_of(1 + near, member, last) for member in others])

    def drain(phase):
        for with_far in (False, True):
            for with_near in (True,) if has_near is True else (False, True):
                count = local * len(others)
                count += (with_far + with_near) * local * (1 + len(others))

                @pl.when(jnp.logical_and(has_far == with_far, has_near == with_near))
                def _(count=count):
                    here = near_ref.at[pl.ds(0, count)]
                    pltpu.make_async_remote_copy(
                        src_ref=here,
                        dst_ref=here,
                        send_sem=send_sem.at[phase],
                        recv_sem=send_sem.at[phase],
                        device_id=(img, others[0]),
                        device_id_type=MESH,
                    ).wait_send()

    def mass_at(source, member):
        count = 3 - abs(source)
        base = {0: 0, -1: 3, 1: 5, -2: 7, 2: 8}[source] * blk_count
        return base + member * count, count

    for source in range(-2, 3):
        if source != 0:
            @pl.when(jnp.logical_not(exists(source)))
            def _(source=source):
                first = mass_at(source, 0)[0]
                count = mass_at(source, blk_count)[0] - first
                for sweep in range(ITERS):
                    mass_in[sweep, pl.ds(first, count)] = jnp.zeros(
                        (count, group, block), jnp.float32
                    )
    for source in (-1, 1):
        @pl.when(jnp.logical_not(exists(source)))
        def _(source=source):
            for r in range(local):
                for spot in range(group):
                    dots[r, (1 + source) * group + spot] = jnp.zeros((block, block), jnp.float32)

    small_loads[0].wait()
    pl.semaphore_wait(
        barrier, len(others) + jnp.int32(has_far) + jnp.int32(has_near)
    )
    send_own(0, lambda place: desc_ref.at[place])
    for load in small_loads[1:]:
        load.wait()
    weight_load.wait()

    lanes = lax.broadcasted_iota(jnp.int32, (1, block), 1)
    rows_at = lax.broadcasted_iota(jnp.int32, (block, 1), 0)
    head_of = lax.broadcasted_iota(jnp.int32, (1, width), 1) // head_dim
    own_kpt = [kpt_ref[(img * blk_count + blk) * local + r] for r in range(local)]
    near_ids = [
        [jnp.clip(cov_ref[r, t] - first_block, 0, 3 * group - 1) for t in range(tiles)]
        for r in range(local)
    ]
    limits = [
        [
            jnp.where(t < count_ref[r], kpt_ref[jnp.clip(cov_ref[r, t], 0, kpt_ref.shape[0] - 1)], 0)
            for t in range(tiles)
        ]
        for r in range(local)
    ]
    biases = [
        [jnp.where(lanes < limits[r][t], 0.0, DEAD) for t in range(tiles)] for r in range(local)
    ]
    for r in range(local):
        for spot in range(3 * group):
            limit = 0
            for t in range(tiles):
                limit = jnp.where(near_ids[r][t] == spot, limits[r][t], limit)
            slot_limit[r, spot] = limit

    own = desc_ref[...].reshape(local * block, width)
    query = jnp.dot(own, weight(0), preferred_element_type=jnp.float32).astype(jnp.bfloat16)
    for r in range(local):
        q = query[r * block : (r + 1) * block]
        turned = lax.dot_general(
            jnp.concatenate(
                [jnp.where(head_of == head, q, jnp.zeros_like(q)) for head in range(HEADS)], axis=0
            ),
            weight(1),
            (((1,), (1,)), ((), ())),
            preferred_element_type=jnp.float32,
        )
        spans[r] = (turned * (math.log2(math.e) / math.sqrt(head_dim))).astype(jnp.bfloat16)
    value_turned[...] = weight(2).T
    columns = deep // width
    for column in range(columns):
        merged[:, pl.ds(column * width, width)] = jnp.dot(
            own, merge_part(0, column), preferred_element_type=jnp.float32
        )
    places_at = lax.broadcasted_iota(jnp.int32, (block, block), 0)
    step_heads = 2 if HEADS % 2 == 0 else 1

    def attend(rows, spots, first=False):
        values = lax.dot_general(
            value_turned[...], rows, (((1,), (1,)), ((), ())), preferred_element_type=jnp.float32
        ).astype(jnp.bfloat16)
        lives = [[places_at < slot_limit[r, spot] for spot in spots] for r in range(local)]
        chains = [(r, base) for r in range(local) for base in range(0, HEADS, step_heads)]

        def compare(chain):
            r, base = chain
            logits = lax.dot_general(
                rows,
                spans[r, pl.ds(base * block, step_heads * block)],
                (((1,), (1,)), ((), ())),
                preferred_element_type=jnp.float32,
            )
            tops = []
            for head in range(step_heads):
                top = None
                for place, alive in enumerate(lives[r]):
                    where_to = (pl.ds(place * block, block), pl.ds(head * block, block))
                    part = jnp.where(
                        alive,
                        logits[
                            place * block : (place + 1) * block,
                            head * block : (head + 1) * block,
                        ],
                        DEAD,
                    )
                    logit_ref[r, base // step_heads, where_to[0], where_to[1]] = part
                    top = part if top is None else jnp.maximum(top, part)
                tops.append(jnp.max(top, axis=0, keepdims=True))
            return tops

        def soften(chain, logits):
            r, base = chain
            weights = []
            scales = []
            for head in range(step_heads):
                where_to = pl.ds(base + head, 1)
                parts = [
                    logit_ref[
                        r,
                        base // step_heads,
                        pl.ds(place * block, block),
                        pl.ds(head * block, block),
                    ]
                    for place in range(len(spots))
                ]
                top = logits[head]
                if not first:
                    old = top_ref[r, where_to, :]
                    top = jnp.maximum(top, old)
                    scales.append(jnp.exp2(old - top))
                parts = [jnp.exp2(part - top) for part in parts]
                total = jnp.sum(functools.reduce(jnp.add, parts), axis=0, keepdims=True)
                if not first:
                    total = total + sum_ref[r, where_to, :] * scales[head]
                top_ref[r, where_to, :] = top
                sum_ref[r, where_to, :] = total
                weights.append(
                    jnp.concatenate([part.astype(jnp.bfloat16) for part in parts], axis=0)
                )
            return jnp.concatenate(weights, axis=1), scales

        def blend(chain, weights, scales):
            r, base = chain
            out = jnp.dot(
                values[base * head_dim : (base + step_heads) * head_dim],
                weights,
                preferred_element_type=jnp.float32,
            )
            for head in range(step_heads):
                where_to = pl.ds((base + head) * head_dim, head_dim)
                mix = out[
                    head * head_dim : (head + 1) * head_dim, head * block : (head + 1) * block
                ]
                if not first:
                    mix = mix + mix_ref[r, where_to, :] * scales[head]
                mix_ref[r, where_to, :] = mix

        compared = [compare(chain) for chain in chains]
        softened = [soften(chain, logits) for chain, logits in zip(chains, compared)]
        for chain, soft in zip(chains, softened):
            blend(chain, *soft)

    def attend_near(spots):
        attend(jnp.concatenate([near_desc[spot] for spot in spots], axis=0), spots)

    attend(own, [slot_of(1, blk, place) for place in range(local)], first=True)
    collect(0, attend_near)

    message = jnp.concatenate(
        [
            jnp.concatenate(
                [
                    mix_ref[r, pl.ds(head * head_dim, head_dim), :]
                    * (1.0 / sum_ref[r, pl.ds(head, 1), :])
                    for head in range(HEADS)
                ],
                axis=0,
            )
            for r in range(local)
        ],
        axis=1,
    ).astype(jnp.bfloat16)
    refined = desc_ref[...].reshape(local * block, width).astype(jnp.float32)
    for column in range(columns):
        hidden = jnp.maximum(
            merged[:, pl.ds(column * width, width)]
            + lax.dot_general(
                message,
                merge_part(1, column),
                (((0,), (0,)), ((), ())),
                preferred_element_type=jnp.float32,
            ),
            0.0,
        ).astype(jnp.bfloat16)
        refined = refined + jnp.dot(
            hidden,
            weights_ref[pl.ds(starts[3] + column * width, width), :],
            preferred_element_type=jnp.float32,
        )
    refined = refined.astype(jnp.bfloat16)
    near_ref[pl.ds(slot_of(1, blk, 0), local)] = refined.reshape(local, block, width)
    send_own(1, lambda place: near_ref.at[slot_of(1, blk, place)])

    mine = refined * jnp.asarray(1.0 / math.sqrt(width), jnp.bfloat16)

    def multiply(spots):
        theirs = jnp.concatenate([near_ref[spot] for spot in spots], axis=0)
        out = lax.dot_general(
            mine, theirs, (((1,), (1,)), ((), ())), preferred_element_type=jnp.float32
        )
        for r in range(local):
            for place, spot in enumerate(spots):
                dots[r, spot] = LOG2E * out[
                    r * block : (r + 1) * block, place * block : (place + 1) * block
                ]

    multiply([slot_of(1, blk, place) for place in range(local)])
    collect(1, multiply)

    dust = dust_ref[0]
    dust2 = dust * LOG2E
    row_live = [rows_at < own_kpt[r] for r in range(local)]
    row_bias = [jnp.where(row_live[r], 0.0, DEAD) for r in range(local)]

    slots = lax.broadcasted_iota(jnp.int32, (group, 1), 0)
    pots = [jnp.zeros((group, block), jnp.float32)] * 3

    def mass_start(sweep, shift, member):
        first, count = mass_at(-shift, blk)
        pltpu.make_async_remote_copy(
            src_ref=acc.at[sweep, pl.ds(max(0, shift), count)],
            dst_ref=mass_in.at[sweep, pl.ds(first, count)],
            send_sem=mass_ssem.at[sweep],
            recv_sem=mass_rsem.at[sweep],
            device_id=(img + shift, member),
            device_id_type=MESH,
        ).start()

    def mass_wait(sweep, wait):
        for below in range(3):
            for above in range(3):
                count = 3 * len(others)
                for reach in (below, above):
                    count += sum((3 - step) * blk_count for step in range(1, reach + 1))

                @pl.when(
                    jnp.logical_and(
                        jnp.minimum(img, 2) == below,
                        jnp.minimum(img_count - 1 - img, 2) == above,
                    )
                )
                def _(count=count):
                    here = mass_in.at[sweep, pl.ds(0, count)]
                    wait(
                        pltpu.make_async_remote_copy(
                            src_ref=here,
                            dst_ref=here,
                            send_sem=mass_ssem.at[sweep],
                            recv_sem=mass_rsem.at[sweep],
                            device_id=(img, others[0]),
                            device_id_type=MESH,
                        )
                    )

    def each_partner(body):
        for shift in (-1, 1, -2, 2):
            def run(shift=shift):
                for member in range(blk_count):
                    body(shift, member)
            pl.when(exists(shift))(run)
        for member in others:
            body(0, member)

    row_pots = [None] * local
    for sweep in range(ITERS):
        spread = [jnp.zeros((group, block), jnp.float32)] * 3
        for r in range(local):
            top = None
            for t in range(tiles):
                if sweep == 0:
                    moved = dots[r, near_ids[r][t]] + (row_bias[r] + biases[r][t])
                    scores[r, t] = moved
                else:
                    moved = scores[r, t] + pot[pl.ds(near_ids[r][t], 1), :]
                    shifted[r, t] = moved
                top = moved if t == 0 else jnp.maximum(top, moved)
            held = scores if sweep == 0 else shifted
            top = jnp.maximum(jnp.max(top, axis=1, keepdims=True), dust2)
            terms = [jnp.exp2(held[r, t] - top) for t in range(tiles)]
            total = functools.reduce(jnp.add, terms)
            total = jnp.sum(total, axis=1, keepdims=True) + jnp.exp2(dust2 - top)
            row_pots[r] = -(top + jnp.log2(total))
            inverse = 1.0 / total
            for t in range(tiles):
                mass = jnp.sum(terms[t] * inverse, axis=0, keepdims=True)
                for section in range(3):
                    hit = slots == near_ids[r][t] - section * group
                    spread[section] = spread[section] + jnp.where(hit, mass, 0.0)
        for section in range(3):
            acc[sweep, section] = spread[section]
        each_partner(lambda shift, member: mass_start(sweep, shift, member))
        if sweep == 0:
            drain(0)
            drain(1)
        if sweep == ITERS - 1:
            for r in range(local):
                row = jnp.broadcast_to(row_pots[r] * LN2, (block, block))
                row = jnp.sum(jnp.where(rows_at == lanes, row, 0.0), axis=0, keepdims=True)
                tail_ref[pl.ds(local * tiles + r, 1), :] = jnp.where(lanes < own_kpt[r], dust + row, 0.0)
                for t in range(tiles):
                    scores[r, t] = (scores[r, t] + row_pots[r]) * LN2
        sums = list(spread)
        mass_wait(sweep, lambda copy: copy.wait_recv())
        for source in range(-2, 3):
            for member in others if source == 0 else range(blk_count):
                for section in range(max(0, source), 3 + min(0, source)):
                    first, _ = mass_at(source, member)
                    sums[section] = sums[section] + mass_in[
                        sweep, first + section - max(0, source)
                    ]
        for section in range(3):
            pots[section] = pots[section] - jnp.log2(
                sums[section] + jnp.exp2(dust2 + pots[section])
            )
            pot[pl.ds(section * group, group), :] = (
                pots[section] * LN2 if sweep == ITERS - 1 else pots[section]
            )

    for r in range(local):
        for t in range(tiles):
            tail_ref[pl.ds(r * tiles + t, 1), :] = pot[pl.ds(near_ids[r][t], 1), :]
        mine = pot[pl.ds(group + blk * local + r, 1), :]
        tail_ref[pl.ds(local * (tiles + 1) + r, 1), :] = jnp.where(lanes < own_kpt[r], dust + mine, 0.0)
    for sweep in range(ITERS):
        mass_wait(sweep, lambda copy: copy.wait_send())


def finish(base_ref, tail_ref, plan_out, row_out, col_out, made, out_sem, end_sem):
    local, tiles = base_ref.shape[:2]
    places = [(r, t) for r in range(local) for t in range(tiles)]

    def put(r, t):
        return pltpu.make_async_copy(made.at[r, t], plan_out.at[r, t], out_sem)

    ends = [
        pltpu.make_async_copy(
            tail_ref.at[pl.ds(local * (tiles + step), local)], target, end_sem.at[step]
        )
        for step, target in enumerate((row_out, col_out))
    ]
    for end in ends:
        end.start()
    for r, t in places:
        base = base_ref[r, t]
        out = base + tail_ref[pl.ds(r * tiles + t, 1), :]
        made[r, t] = jnp.where(base > 0.1 * DEAD, out, 0.0)
        put(r, t).start()
    for end in ends:
        end.wait()
    pltpu.make_async_copy(made, plan_out, out_sem).wait()


def on_device(
    img_count,
    blk_count,
    descriptors,
    covisible,
    tile_counts,
    keypoints,
    query_weight,
    key_weight,
    value_weight,
    merge_weight,
    output_weight,
    dustbin,
):
    local, block, width = descriptors.shape
    tiles = covisible.shape[1]
    group = local * blk_count
    near = 3 * group
    most = max(local * (blk_count - 1), (local - 1) * blk_count + 1, blk_count, local)
    pace = 2 if HEADS % 2 == 0 else 1
    weight_rows = (
        3 * width
        + output_weight.shape[0]
        + merge_weight.shape[0] * (merge_weight.shape[1] // width)
    )
    vmem = pl.BlockSpec(memory_space=pltpu.VMEM)
    hbm = pl.BlockSpec(memory_space=pltpu.HBM)
    dma = pltpu.SemaphoreType.DMA
    half = jnp.bfloat16
    full = jnp.float32
    base, tail = pl.pallas_call(
        functools.partial(kernel, img_count, blk_count),
        out_shape=(
            pltpu.VMEM((local, tiles, block, block), full),
            pltpu.VMEM((local * (tiles + 2), block), full),
        ),
        in_specs=[hbm] * 10,
        out_specs=(vmem, vmem),
        scratch_shapes=[
            pltpu.VMEM(descriptors.shape, half),
            pltpu.SMEM(covisible.shape, jnp.int32),
            pltpu.SMEM(tile_counts.shape, jnp.int32),
            pltpu.SMEM(keypoints.shape, jnp.int32),
            pltpu.SMEM(dustbin.shape, full),
            pltpu.VMEM((weight_rows, width), half),
            dma((6,)),
            pltpu.VMEM((near, block, width), half),
            pltpu.VMEM((near, block, width), half),
            pltpu.VMEM(value_weight.shape, half),
            pltpu.VMEM((local, HEADS * block, width), half),
            pltpu.VMEM((local * block, merge_weight.shape[1]), full),
            pltpu.SMEM((local, near), jnp.int32),
            pltpu.VMEM((local, HEADS, block), full),
            pltpu.VMEM((local, HEADS, block), full),
            pltpu.VMEM((local, width, block), full),
            pltpu.VMEM((local, HEADS // pace, most * block, pace * block), full),
            pltpu.VMEM((local, near, block, block), full),
            pltpu.VMEM((local, tiles, block, block), full),
            pltpu.VMEM((ITERS, 3, group, block), full),
            pltpu.VMEM((ITERS, 9 * blk_count, group, block), full),
            pltpu.VMEM((near, block), full),
            dma((2,)),
            dma((2,)),
            dma((2, 2, local)),
            dma((2, 2, local)),
            dma((ITERS,)),
            dma((ITERS,)),
        ],
        compiler_params=pltpu.CompilerParams(
            collective_id=0, has_side_effects=True, vmem_limit_bytes=VMEM_BYTES
        ),
    )(
        *(
            pltpu.with_memory_space_constraint(x, pltpu.HBM)
            for x in (
                descriptors,
                covisible,
                tile_counts,
                keypoints,
                query_weight,
                key_weight,
                value_weight,
                merge_weight,
                output_weight,
            )
        ),
        dustbin,
    )
    return pl.pallas_call(
        finish,
        out_shape=(
            jax.ShapeDtypeStruct(base.shape, full),
            jax.ShapeDtypeStruct((local, block), full),
            jax.ShapeDtypeStruct((local, block), full),
        ),
        in_specs=[vmem, vmem],
        out_specs=(hbm, hbm, hbm),
        scratch_shapes=[
            pltpu.VMEM(base.shape, full),
            dma,
            dma((2,)),
        ],
        compiler_params=pltpu.CompilerParams(vmem_limit_bytes=VMEM_BYTES),
    )(*(pltpu.with_memory_space_constraint(x, pltpu.VMEM) for x in (base, tail)))


def solution(mesh):
    in_specs = (
        P(("img", "blk"), None, None),
        P(("img", "blk"), None),
        P(("img", "blk")),
        P(),
        P(),
        P(),
        P(),
        P(),
        P(),
        P(),
    )
    out_specs = (
        P(("img", "blk"), None, None, None),
        P(("img", "blk"), None),
        P(("img", "blk"), None),
    )
    return jax.shard_map(
        functools.partial(on_device, mesh.shape["img"], mesh.shape["blk"]),
        mesh=mesh,
        in_specs=in_specs,
        out_specs=out_specs,
        check_vma=False,
    )
```

```python
import functools
import math

import jax
import jax.numpy as jnp
from jax import lax
from jax.experimental import pallas as pl
from jax.experimental.pallas import tpu as pltpu
from jax.sharding import PartitionSpec as P

HEADS = 4
ITERS = 3
DEAD = -1e30
LOG2E = math.log2(math.e)
LN2 = math.log(2.0)
MESH = pl.DeviceIdType.MESH
VMEM_BYTES = 48 * 1024 * 1024


def kernel(
    img_count,
    blk_count,
    desc_in,
    cov_in,
    count_in,
    kpt_in,
    wq_in,
    wk_in,
    wv_in,
    wm_in,
    wo_in,
    dust_in,
    scores,
    tail_ref,
    desc_ref,
    cov_ref,
    count_ref,
    kpt_ref,
    dust_ref,
    weights_ref,
    load_sem,
    near_desc,
    near_ref,
    value_turned,
    spans,
    merged,
    slot_limit,
    top_ref,
    sum_ref,
    mix_ref,
    logit_ref,
    dots,
    shifted,
    acc,
    mass_in,
    pot,
    send_sem,
    pair_sem,
    direct_sem,
    passed_sem,
    mass_ssem,
    mass_rsem,
):
    local, block, width = desc_ref.shape
    tiles = cov_ref.shape[1]
    group = local * blk_count
    head_dim = width // HEADS
    deep = wm_in.shape[1]
    img = lax.axis_index("img")
    blk = lax.axis_index("blk")
    others = [lax.rem(blk + step, blk_count) for step in range(1, blk_count)]
    first_block = (img - 1) * group
    far = 2 * lax.rem(img, 2) - 1
    near = -far

    def exists(shift):
        if isinstance(shift, int):
            return img + shift < img_count if shift > 0 else img + shift >= 0
        return jnp.logical_and(img + shift >= 0, img + shift < img_count)

    has_far = exists(far)
    has_near = True if img_count % 2 == 0 else exists(near)

    def when(condition):
        return (lambda body: body()) if condition is True else pl.when(condition)


    sizes = (width, width, width, deep)
    starts = [sum(sizes[:place]) for place in range(len(sizes) + 1)]
    weight_rows = [(wq_in, 0), (wk_in, 0), (wv_in, 0), (wo_in, 0)]
    weight_rows += [(wm_in, column) for column in range(0, deep, width)]
    loads = []
    start = 0
    for source, column in weight_rows:
        count = source.shape[0]
        loads.append(
            pltpu.make_async_copy(
                source.at[:, pl.ds(column, width)],
                weights_ref.at[pl.ds(start, count)],
                load_sem.at[0],
            )
        )
        start += count
    weight_load = pltpu.make_async_copy(weights_ref, weights_ref, load_sem.at[0])
    small_loads = [
        pltpu.make_async_copy(source, target, load_sem.at[1 + place])
        for place, (source, target) in enumerate(
            (
                (desc_in, desc_ref),
                (cov_in, cov_ref),
                (count_in, count_ref),
                (kpt_in, kpt_ref),
            )
        )
    ]

    def weight(place):
        return weights_ref[pl.ds(starts[place], sizes[place]), :]

    def merge_part(step, column):
        first = starts[4] + column * 2 * width + step * width
        return weights_ref[pl.ds(first, width), :]

    barrier = pltpu.get_barrier_semaphore()

    def greet(shift, member):
        pl.semaphore_signal(
            barrier, inc=1, device_id=(img + shift, member), device_id_type=MESH
        )

    when(has_far)(lambda: greet(far, blk))
    when(has_near)(lambda: greet(near, blk))
    for member in others:
        greet(0, member)

    for load in small_loads + loads:
        load.start()

    def slot_of(section, member, place):
        return (section * blk_count + member) * local + place

    def push(phase, source, slot, rsem, device):
        room = (near_desc, near_ref)[phase]
        pltpu.make_async_remote_copy(
            src_ref=source,
            dst_ref=room.at[slot],
            send_sem=send_sem.at[phase],
            recv_sem=rsem,
            device_id=device,
            device_id_type=MESH,
        ).start()

    def received(phase, rsem, first, count):
        room = (near_desc, near_ref)[phase]
        here = room.at[pl.ds(first, count)]
        pltpu.make_async_remote_copy(
            src_ref=here,
            dst_ref=here,
            send_sem=send_sem.at[phase],
            recv_sem=rsem,
            device_id=(img, others[0]),
            device_id_type=MESH,
        ).wait_recv()

    sides = ((has_far, far), (has_near, near))

    def send_own(phase, source):
        for place in range(local):
            for member in others:
                push(
                    phase,
                    source(place),
                    slot_of(1, blk, place),
                    pair_sem.at[phase],
                    (img, member),
                )
        for order, (there, shift) in enumerate(sides):
            @when(there)
            def _(order=order, shift=shift):
                for place in range(local):
                    push(
                        phase,
                        source(place),
                        slot_of(1 - shift, blk, place),
                        direct_sem.at[phase, order, place],
                        (img + shift, blk),
                    )

    def collect(phase, use):
        room = (near_desc, near_ref)[phase]
        count = len(others)

        def relay(order, place):
            slot = slot_of(1 + sides[order][1], blk, place)
            received(phase, direct_sem.at[phase, order, place], slot, 1)
            for member in others:
                push(
                    phase, room.at[slot], slot, passed_sem.at[phase, order, place], (img, member)
                )

        def passed(order, place):
            section = 1 + sides[order][1]
            first = slot_of(section, others[0], place) if count == 1 else 0
            received(phase, passed_sem.at[phase, order, place], first, count)
            return [slot_of(section, member, place) for member in range(blk_count)]

        def piece(order, place):
            use(passed(order, place))

        first = slot_of(1, others[0], 0) if count == 1 else 0
        received(phase, pair_sem.at[phase], first, count * local)
        use([slot_of(1, member, place) for member in others for place in range(local)])

        @pl.when(has_far)
        def _():
            for place in range(local):
                relay(0, place)
            for place in range(local - 1):
                piece(0, place)

        @when(has_near)
        def _():
            for place in range(local - 1):
                relay(1, place)

        @pl.when(has_far)
        def _():
            piece(0, local - 1)

        @when(has_near)
        def _():
            last = local - 1
            relay(1, last)
            spots = [slot_of(1 + near, blk, last)]
            for place in range(last):
                spots += passed(1, place)
            use(spots)
            passed(1, last)
            use([slot_of(1 + near, member, last) for member in others])

    def drain(phase):
        for with_far in (False, True):
            for with_near in (True,) if has_near is True else (False, True):
                count = local * len(others)
                count += (with_far + with_near) * local * (1 + len(others))

                @pl.when(jnp.logical_and(has_far == with_far, has_near == with_near))
                def _(count=count):
                    here = near_ref.at[pl.ds(0, count)]
                    pltpu.make_async_remote_copy(
                        src_ref=here,
                        dst_ref=here,
                        send_sem=send_sem.at[phase],
                        recv_sem=send_sem.at[phase],
                        device_id=(img, others[0]),
                        device_id_type=MESH,
                    ).wait_send()

    def mass_at(source, member):
        count = 3 - abs(source)
        base = {0: 0, -1: 3, 1: 5, -2: 7, 2: 8}[source] * blk_count
        return base + member * count, count

    for source in range(-2, 3):
        if source != 0:
            @pl.when(jnp.logical_not(exists(source)))
            def _(source=source):
                first = mass_at(source, 0)[0]
                count = mass_at(source, blk_count)[0] - first
                for sweep in range(ITERS):
                    mass_in[sweep, pl.ds(first, count)] = jnp.zeros(
                        (count, group, block), jnp.float32
                    )
    for source in (-1, 1):
        @pl.when(jnp.logical_not(exists(source)))
        def _(source=source):
            for r in range(local):
                for spot in range(group):
                    dots[r, (1 + source) * group + spot] = jnp.zeros((block, block), jnp.float32)

    small_loads[0].wait()
    pl.semaphore_wait(
        barrier, len(others) + jnp.int32(has_far) + jnp.int32(has_near)
    )
    send_own(0, lambda place: desc_ref.at[place])
    for load in small_loads[1:]:
        load.wait()
    weight_load.wait()

    lanes = lax.broadcasted_iota(jnp.int32, (1, block), 1)
    rows_at = lax.broadcasted_iota(jnp.int32, (block, 1), 0)
    head_of = lax.broadcasted_iota(jnp.int32, (1, width), 1) // head_dim
    own_kpt = [kpt_ref[(img * blk_count + blk) * local + r] for r in range(local)]
    near_ids = [
        [jnp.clip(cov_ref[r, t] - first_block, 0, 3 * group - 1) for t in range(tiles)]
        for r in range(local)
    ]
    limits = [
        [
            jnp.where(t < count_ref[r], kpt_ref[jnp.clip(cov_ref[r, t], 0, kpt_ref.shape[0] - 1)], 0)
            for t in range(tiles)
        ]
        for r in range(local)
    ]
    biases = [
        [jnp.where(lanes < limits[r][t], 0.0, DEAD) for t in range(tiles)] for r in range(local)
    ]
    for r in range(local):
        for spot in range(3 * group):
            limit = 0
            for t in range(tiles):
                limit = jnp.where(near_ids[r][t] == spot, limits[r][t], limit)
            slot_limit[r, spot] = limit

    own = desc_ref[...].reshape(local * block, width)
    query = jnp.dot(own, weight(0), preferred_element_type=jnp.float32).astype(jnp.bfloat16)
    for r in range(local):
        q = query[r * block : (r + 1) * block]
        turned = lax.dot_general(
            jnp.concatenate(
                [jnp.where(head_of == head, q, jnp.zeros_like(q)) for head in range(HEADS)], axis=0
            ),
            weight(1),
            (((1,), (1,)), ((), ())),
            preferred_element_type=jnp.float32,
        )
        spans[r] = (turned * (math.log2(math.e) / math.sqrt(head_dim))).astype(jnp.bfloat16)
    value_turned[...] = weight(2).T
    columns = deep // width
    for column in range(columns):
        merged[:, pl.ds(column * width, width)] = jnp.dot(
            own, merge_part(0, column), preferred_element_type=jnp.float32
        )
    places_at = lax.broadcasted_iota(jnp.int32, (block, block), 0)
    step_heads = 2 if HEADS % 2 == 0 else 1

    def attend(rows, spots, first=False):
        values = lax.dot_general(
            value_turned[...], rows, (((1,), (1,)), ((), ())), preferred_element_type=jnp.float32
        ).astype(jnp.bfloat16)
        lives = [[places_at < slot_limit[r, spot] for spot in spots] for r in range(local)]
        chains = [(r, base) for r in range(local) for base in range(0, HEADS, step_heads)]

        def compare(chain):
            r, base = chain
            logits = lax.dot_general(
                rows,
                spans[r, pl.ds(base * block, step_heads * block)],
                (((1,), (1,)), ((), ())),
                preferred_element_type=jnp.float32,
            )
            tops = []
            for head in range(step_heads):
                top = None
                for place, alive in enumerate(lives[r]):
                    where_to = (pl.ds(place * block, block), pl.ds(head * block, block))
                    part = jnp.where(
                        alive,
                        logits[
                            place * block : (place + 1) * block,
                            head * block : (head + 1) * block,
                        ],
                        DEAD,
                    )
                    logit_ref[r, base // step_heads, where_to[0], where_to[1]] = part
                    top = part if top is None else jnp.maximum(top, part)
                tops.append(jnp.max(top, axis=0, keepdims=True))
            return tops

        def soften(chain, logits):
            r, base = chain
            weights = []
            scales = []
            for head in range(step_heads):
                where_to = pl.ds(base + head, 1)
                parts = [
                    logit_ref[
                        r,
                        base // step_heads,
                        pl.ds(place * block, block),
                        pl.ds(head * block, block),
                    ]
                    for place in range(len(spots))
                ]
                top = logits[head]
                if not first:
                    old = top_ref[r, where_to, :]
                    top = jnp.maximum(top, old)
                    scales.append(jnp.exp2(old - top))
                parts = [jnp.exp2(part - top) for part in parts]
                total = jnp.sum(functools.reduce(jnp.add, parts), axis=0, keepdims=True)
                if not first:
                    total = total + sum_ref[r, where_to, :] * scales[head]
                top_ref[r, where_to, :] = top
                sum_ref[r, where_to, :] = total
                weights.append(
                    jnp.concatenate([part.astype(jnp.bfloat16) for part in parts], axis=0)
                )
            return jnp.concatenate(weights, axis=1), scales

        def blend(chain, weights, scales):
            r, base = chain
            out = jnp.dot(
                values[base * head_dim : (base + step_heads) * head_dim],
                weights,
                preferred_element_type=jnp.float32,
            )
            for head in range(step_heads):
                where_to = pl.ds((base + head) * head_dim, head_dim)
                mix = out[
                    head * head_dim : (head + 1) * head_dim, head * block : (head + 1) * block
                ]
                if not first:
                    mix = mix + mix_ref[r, where_to, :] * scales[head]
                mix_ref[r, where_to, :] = mix

        compared = [compare(chain) for chain in chains]
        softened = [soften(chain, logits) for chain, logits in zip(chains, compared)]
        for chain, soft in zip(chains, softened):
            blend(chain, *soft)

    def attend_near(spots):
        attend(jnp.concatenate([near_desc[spot] for spot in spots], axis=0), spots)

    attend(own, [slot_of(1, blk, place) for place in range(local)], first=True)
    collect(0, attend_near)

    message = jnp.concatenate(
        [
            jnp.concatenate(
                [
                    mix_ref[r, pl.ds(head * head_dim, head_dim), :]
                    * (1.0 / sum_ref[r, pl.ds(head, 1), :])
                    for head in range(HEADS)
                ],
                axis=0,
            )
            for r in range(local)
        ],
        axis=1,
    ).astype(jnp.bfloat16)
    refined = desc_ref[...].reshape(local * block, width).astype(jnp.float32)
    for column in range(columns):
        hidden = jnp.maximum(
            merged[:, pl.ds(column * width, width)]
            + lax.dot_general(
                message,
                merge_part(1, column),
                (((0,), (0,)), ((), ())),
                preferred_element_type=jnp.float32,
            ),
            0.0,
        ).astype(jnp.bfloat16)
        refined = refined + jnp.dot(
            hidden,
            weights_ref[pl.ds(starts[3] + column * width, width), :],
            preferred_element_type=jnp.float32,
        )
    refined = refined.astype(jnp.bfloat16)
    near_ref[pl.ds(slot_of(1, blk, 0), local)] = refined.reshape(local, block, width)
    send_own(1, lambda place: near_ref.at[slot_of(1, blk, place)])

    mine = refined * jnp.asarray(1.0 / math.sqrt(width), jnp.bfloat16)

    def multiply(spots):
        theirs = jnp.concatenate([near_ref[spot] for spot in spots], axis=0)
        out = lax.dot_general(
            mine, theirs, (((1,), (1,)), ((), ())), preferred_element_type=jnp.float32
        )
        for r in range(local):
            for place, spot in enumerate(spots):
                dots[r, spot] = LOG2E * out[
                    r * block : (r + 1) * block, place * block : (place + 1) * block
                ]

    multiply([slot_of(1, blk, place) for place in range(local)])
    collect(1, multiply)

    dust = dust_in[0]
    dust2 = dust * LOG2E
    row_live = [rows_at < own_kpt[r] for r in range(local)]
    row_bias = [jnp.where(row_live[r], 0.0, DEAD) for r in range(local)]

    slots = lax.broadcasted_iota(jnp.int32, (group, 1), 0)
    pots = [jnp.zeros((group, block), jnp.float32)] * 3

    def mass_start(sweep, shift, member):
        first, count = mass_at(-shift, blk)
        pltpu.make_async_remote_copy(
            src_ref=acc.at[sweep, pl.ds(max(0, shift), count)],
            dst_ref=mass_in.at[sweep, pl.ds(first, count)],
            send_sem=mass_ssem.at[sweep],
            recv_sem=mass_rsem.at[sweep],
            device_id=(img + shift, member),
            device_id_type=MESH,
        ).start()

    def mass_wait(sweep, wait):
        for below in range(3):
            for above in range(3):
                count = 3 * len(others)
                for reach in (below, above):
                    count += sum((3 - step) * blk_count for step in range(1, reach + 1))

                @pl.when(
                    jnp.logical_and(
                        jnp.minimum(img, 2) == below,
                        jnp.minimum(img_count - 1 - img, 2) == above,
                    )
                )
                def _(count=count):
                    here = mass_in.at[sweep, pl.ds(0, count)]
                    wait(
                        pltpu.make_async_remote_copy(
                            src_ref=here,
                            dst_ref=here,
                            send_sem=mass_ssem.at[sweep],
                            recv_sem=mass_rsem.at[sweep],
                            device_id=(img, others[0]),
                            device_id_type=MESH,
                        )
                    )

    def each_partner(body):
        for shift in (-1, 1, -2, 2):
            def run(shift=shift):
                for member in range(blk_count):
                    body(shift, member)
            pl.when(exists(shift))(run)
        for member in others:
            body(0, member)

    row_pots = [None] * local
    for sweep in range(ITERS):
        spread = [jnp.zeros((group, block), jnp.float32)] * 3
        for r in range(local):
            top = None
            for t in range(tiles):
                if sweep == 0:
                    moved = dots[r, near_ids[r][t]] + (row_bias[r] + biases[r][t])
                    scores[r, t] = moved
                else:
                    moved = scores[r, t] + pot[pl.ds(near_ids[r][t], 1), :]
                    shifted[r, t] = moved
                top = moved if t == 0 else jnp.maximum(top, moved)
            held = scores if sweep == 0 else shifted
            top = jnp.maximum(jnp.max(top, axis=1, keepdims=True), dust2)
            terms = [jnp.exp2(held[r, t] - top) for t in range(tiles)]
            total = functools.reduce(jnp.add, terms)
            total = jnp.sum(total, axis=1, keepdims=True) + jnp.exp2(dust2 - top)
            row_pots[r] = -(top + jnp.log2(total))
            inverse = 1.0 / total
            for t in range(tiles):
                mass = jnp.sum(terms[t] * inverse, axis=0, keepdims=True)
                for section in range(3):
                    hit = slots == near_ids[r][t] - section * group
                    spread[section] = spread[section] + jnp.where(hit, mass, 0.0)
        for section in range(3):
            acc[sweep, section] = spread[section]
        each_partner(lambda shift, member: mass_start(sweep, shift, member))
        if sweep == 0:
            drain(0)
            drain(1)
        if sweep == ITERS - 1:
            for r in range(local):
                row = jnp.broadcast_to(row_pots[r] * LN2, (block, block))
                row = jnp.sum(jnp.where(rows_at == lanes, row, 0.0), axis=0, keepdims=True)
                tail_ref[pl.ds(local * tiles + r, 1), :] = jnp.where(lanes < own_kpt[r], dust + row, 0.0)
                for t in range(tiles):
                    scores[r, t] = (scores[r, t] + row_pots[r]) * LN2
        sums = list(spread)
        mass_wait(sweep, lambda copy: copy.wait_recv())
        for source in range(-2, 3):
            for member in others if source == 0 else range(blk_count):
                for section in range(max(0, source), 3 + min(0, source)):
                    first, _ = mass_at(source, member)
                    sums[section] = sums[section] + mass_in[
                        sweep, first + section - max(0, source)
                    ]
        for section in range(3):
            pots[section] = pots[section] - jnp.log2(
                sums[section] + jnp.exp2(dust2 + pots[section])
            )
            pot[pl.ds(section * group, group), :] = (
                pots[section] * LN2 if sweep == ITERS - 1 else pots[section]
            )

    for r in range(local):
        for t in range(tiles):
            tail_ref[pl.ds(r * tiles + t, 1), :] = pot[pl.ds(near_ids[r][t], 1), :]
        mine = pot[pl.ds(group + blk * local + r, 1), :]
        tail_ref[pl.ds(local * (tiles + 1) + r, 1), :] = jnp.where(lanes < own_kpt[r], dust + mine, 0.0)
    for sweep in range(ITERS):
        mass_wait(sweep, lambda copy: copy.wait_send())


def finish(base_ref, tail_ref, plan_out, row_out, col_out, made, out_sem, end_sem):
    local, tiles = base_ref.shape[:2]
    places = [(r, t) for r in range(local) for t in range(tiles)]

    def put(r, t):
        return pltpu.make_async_copy(made.at[r, t], plan_out.at[r, t], out_sem)

    ends = [
        pltpu.make_async_copy(
            tail_ref.at[pl.ds(local * (tiles + step), local)], target, end_sem.at[step]
        )
        for step, target in enumerate((row_out, col_out))
    ]
    for end in ends:
        end.start()
    for r, t in places:
        base = base_ref[r, t]
        out = base + tail_ref[pl.ds(r * tiles + t, 1), :]
        made[r, t] = jnp.where(base > 0.1 * DEAD, out, 0.0)
        put(r, t).start()
    for end in ends:
        end.wait()
    pltpu.make_async_copy(made, plan_out, out_sem).wait()


def on_device(
    img_count,
    blk_count,
    descriptors,
    covisible,
    tile_counts,
    keypoints,
    query_weight,
    key_weight,
    value_weight,
    merge_weight,
    output_weight,
    dustbin,
):
    local, block, width = descriptors.shape
    tiles = covisible.shape[1]
    group = local * blk_count
    near = 3 * group
    most = max(local * (blk_count - 1), (local - 1) * blk_count + 1, blk_count, local)
    pace = 2 if HEADS % 2 == 0 else 1
    weight_rows = (
        3 * width
        + output_weight.shape[0]
        + merge_weight.shape[0] * (merge_weight.shape[1] // width)
    )
    vmem = pl.BlockSpec(memory_space=pltpu.VMEM)
    hbm = pl.BlockSpec(memory_space=pltpu.HBM)
    dma = pltpu.SemaphoreType.DMA
    half = jnp.bfloat16
    full = jnp.float32
    base, tail = pl.pallas_call(
        functools.partial(kernel, img_count, blk_count),
        out_shape=(
            pltpu.VMEM((local, tiles, block, block), full),
            pltpu.VMEM((local * (tiles + 2), block), full),
        ),
        in_specs=[hbm] * 9 + [pl.BlockSpec(memory_space=pltpu.SMEM)],
        out_specs=(vmem, vmem),
        scratch_shapes=[
            pltpu.VMEM(descriptors.shape, half),
            pltpu.SMEM(covisible.shape, jnp.int32),
            pltpu.SMEM(tile_counts.shape, jnp.int32),
            pltpu.SMEM(keypoints.shape, jnp.int32),
            pltpu.SMEM(dustbin.shape, full),
            pltpu.VMEM((weight_rows, width), half),
            dma((6,)),
            pltpu.VMEM((near, block, width), half),
            pltpu.VMEM((near, block, width), half),
            pltpu.VMEM(value_weight.shape, half),
            pltpu.VMEM((local, HEADS * block, width), half),
            pltpu.VMEM((local * block, merge_weight.shape[1]), full),
            pltpu.SMEM((local, near), jnp.int32),
            pltpu.VMEM((local, HEADS, block), full),
            pltpu.VMEM((local, HEADS, block), full),
            pltpu.VMEM((local, width, block), full),
            pltpu.VMEM((local, HEADS // pace, most * block, pace * block), full),
            pltpu.VMEM((local, near, block, block), full),
            pltpu.VMEM((local, tiles, block, block), full),
            pltpu.VMEM((ITERS, 3, group, block), full),
            pltpu.VMEM((ITERS, 9 * blk_count, group, block), full),
            pltpu.VMEM((near, block), full),
            dma((2,)),
            dma((2,)),
            dma((2, 2, local)),
            dma((2, 2, local)),
            dma((ITERS,)),
            dma((ITERS,)),
        ],
        compiler_params=pltpu.CompilerParams(
            collective_id=0, has_side_effects=True, vmem_limit_bytes=VMEM_BYTES
        ),
    )(
        *(
            pltpu.with_memory_space_constraint(x, pltpu.HBM)
            for x in (
                descriptors,
                covisible,
                tile_counts,
                keypoints,
                query_weight,
                key_weight,
                value_weight,
                merge_weight,
                output_weight,
            )
        ),
        dustbin,
    )
    return pl.pallas_call(
        finish,
        out_shape=(
            jax.ShapeDtypeStruct(base.shape, full),
            jax.ShapeDtypeStruct((local, block), full),
            jax.ShapeDtypeStruct((local, block), full),
        ),
        in_specs=[vmem, vmem],
        out_specs=(hbm, hbm, hbm),
        scratch_shapes=[
            pltpu.VMEM(base.shape, full),
            dma,
            dma((2,)),
        ],
        compiler_params=pltpu.CompilerParams(vmem_limit_bytes=VMEM_BYTES),
    )(*(pltpu.with_memory_space_constraint(x, pltpu.VMEM) for x in (base, tail)))


def solution(mesh):
    in_specs = (
        P(("img", "blk"), None, None),
        P(("img", "blk"), None),
        P(("img", "blk")),
        P(),
        P(),
        P(),
        P(),
        P(),
        P(),
        P(),
    )
    out_specs = (
        P(("img", "blk"), None, None, None),
        P(("img", "blk"), None),
        P(("img", "blk"), None),
    )
    return jax.shard_map(
        functools.partial(on_device, mesh.shape["img"], mesh.shape["blk"]),
        mesh=mesh,
        in_specs=in_specs,
        out_specs=out_specs,
        check_vma=False,
    )
```

```python
import functools
import math

import jax
import jax.numpy as jnp
from jax import lax
from jax.experimental import pallas as pl
from jax.experimental.pallas import tpu as pltpu
from jax.sharding import PartitionSpec as P

HEADS = 4
ITERS = 3
DEAD = -1e30
LOG2E = math.log2(math.e)
LN2 = math.log(2.0)
MESH = pl.DeviceIdType.MESH
VMEM_BYTES = 48 * 1024 * 1024


def kernel(
    img_count,
    blk_count,
    desc_in,
    cov_in,
    count_in,
    kpt_in,
    wq_in,
    wk_in,
    wv_in,
    wm_in,
    wo_in,
    dust_in,
    scores,
    tail_ref,
    desc_ref,
    cov_ref,
    count_ref,
    kpt_ref,
    dust_ref,
    weights_ref,
    load_sem,
    near_desc,
    near_ref,
    value_turned,
    spans,
    merged,
    slot_limit,
    top_ref,
    sum_ref,
    mix_ref,
    logit_ref,
    dots,
    shifted,
    acc,
    mass_in,
    pot,
    send_sem,
    pair_sem,
    direct_sem,
    passed_sem,
    mass_ssem,
    mass_rsem,
):
    local, block, width = desc_ref.shape
    tiles = cov_ref.shape[1]
    group = local * blk_count
    head_dim = width // HEADS
    deep = wm_in.shape[1]
    img = lax.axis_index("img")
    blk = lax.axis_index("blk")
    others = [lax.rem(blk + step, blk_count) for step in range(1, blk_count)]
    first_block = (img - 1) * group
    far = 2 * lax.rem(img, 2) - 1
    near = -far

    def exists(shift):
        if isinstance(shift, int):
            return img + shift < img_count if shift > 0 else img + shift >= 0
        return jnp.logical_and(img + shift >= 0, img + shift < img_count)

    has_far = exists(far)
    has_near = True if img_count % 2 == 0 else exists(near)

    def when(condition):
        return (lambda body: body()) if condition is True else pl.when(condition)


    sizes = (width, width, width, deep)
    starts = [sum(sizes[:place]) for place in range(len(sizes) + 1)]
    weight_rows = [(wq_in, 0), (wk_in, 0), (wv_in, 0), (wo_in, 0)]
    weight_rows += [(wm_in, column) for column in range(0, deep, width)]
    loads = []
    start = 0
    for source, column in weight_rows:
        count = source.shape[0]
        loads.append(
            pltpu.make_async_copy(
                source.at[:, pl.ds(column, width)],
                weights_ref.at[pl.ds(start, count)],
                load_sem.at[0],
            )
        )
        start += count
    weight_load = pltpu.make_async_copy(weights_ref, weights_ref, load_sem.at[0])
    small_loads = [
        pltpu.make_async_copy(source, target, load_sem.at[1 + place])
        for place, (source, target) in enumerate(
            (
                (desc_in, desc_ref),
                (cov_in, cov_ref),
                (count_in, count_ref),
                (kpt_in, kpt_ref),
            )
        )
    ]

    def weight(place):
        return weights_ref[pl.ds(starts[place], sizes[place]), :]

    def merge_part(step, column):
        first = starts[4] + column * 2 * width + step * width
        return weights_ref[pl.ds(first, width), :]

    barrier = pltpu.get_barrier_semaphore()

    def greet(shift, member):
        pl.semaphore_signal(
            barrier, inc=1, device_id=(img + shift, member), device_id_type=MESH
        )

    when(has_far)(lambda: greet(far, blk))
    when(has_near)(lambda: greet(near, blk))
    for member in others:
        greet(0, member)

    for load in small_loads + loads:
        load.start()

    def slot_of(section, member, place):
        return (section * blk_count + member) * local + place

    def push(phase, source, slot, rsem, device):
        room = (near_desc, near_ref)[phase]
        pltpu.make_async_remote_copy(
            src_ref=source,
            dst_ref=room.at[slot],
            send_sem=send_sem.at[phase],
            recv_sem=rsem,
            device_id=device,
            device_id_type=MESH,
        ).start()

    def received(phase, rsem, first, count):
        room = (near_desc, near_ref)[phase]
        here = room.at[pl.ds(first, count)]
        pltpu.make_async_remote_copy(
            src_ref=here,
            dst_ref=here,
            send_sem=send_sem.at[phase],
            recv_sem=rsem,
            device_id=(img, others[0]),
            device_id_type=MESH,
        ).wait_recv()

    sides = ((has_far, far), (has_near, near))

    def send_own(phase, source):
        for place in range(local):
            for member in others:
                push(
                    phase,
                    source(place),
                    slot_of(1, blk, place),
                    pair_sem.at[phase],
                    (img, member),
                )
        for order, (there, shift) in enumerate(sides):
            @when(there)
            def _(order=order, shift=shift):
                for place in range(local):
                    push(
                        phase,
                        source(place),
                        slot_of(1 - shift, blk, place),
                        direct_sem.at[phase, order, place],
                        (img + shift, blk),
                    )

    def collect(phase, use):
        room = (near_desc, near_ref)[phase]
        count = len(others)

        def relay(order, place):
            slot = slot_of(1 + sides[order][1], blk, place)
            received(phase, direct_sem.at[phase, order, place], slot, 1)
            for member in others:
                push(
                    phase, room.at[slot], slot, passed_sem.at[phase, order, place], (img, member)
                )

        def passed(order, place):
            section = 1 + sides[order][1]
            first = slot_of(section, others[0], place) if count == 1 else 0
            received(phase, passed_sem.at[phase, order, place], first, count)
            return [slot_of(section, member, place) for member in range(blk_count)]

        def piece(order, place):
            use(passed(order, place))

        first = slot_of(1, others[0], 0) if count == 1 else 0
        received(phase, pair_sem.at[phase], first, count * local)
        use([slot_of(1, member, place) for member in others for place in range(local)])

        @pl.when(has_far)
        def _():
            for place in range(local):
                relay(0, place)
            for place in range(local - 1):
                piece(0, place)

        @when(has_near)
        def _():
            for place in range(local - 1):
                relay(1, place)

        @pl.when(has_far)
        def _():
            piece(0, local - 1)

        @when(has_near)
        def _():
            last = local - 1
            relay(1, last)
            spots = [slot_of(1 + near, blk, last)]
            for place in range(last):
                spots += passed(1, place)
            use(spots)
            passed(1, last)
            use([slot_of(1 + near, member, last) for member in others])

    def drain(phase):
        for with_far in (False, True):
            for with_near in (True,) if has_near is True else (False, True):
                count = local * len(others)
                count += (with_far + with_near) * local * (1 + len(others))

                @pl.when(jnp.logical_and(has_far == with_far, has_near == with_near))
                def _(count=count):
                    here = near_ref.at[pl.ds(0, count)]
                    pltpu.make_async_remote_copy(
                        src_ref=here,
                        dst_ref=here,
                        send_sem=send_sem.at[phase],
                        recv_sem=send_sem.at[phase],
                        device_id=(img, others[0]),
                        device_id_type=MESH,
                    ).wait_send()

    def mass_at(source, member):
        count = 3 - abs(source)
        base = {0: 0, -1: 3, 1: 5, -2: 7, 2: 8}[source] * blk_count
        return base + member * count, count

    for source in range(-2, 3):
        if source != 0:
            @pl.when(jnp.logical_not(exists(source)))
            def _(source=source):
                first = mass_at(source, 0)[0]
                count = mass_at(source, blk_count)[0] - first
                for sweep in range(ITERS):
                    mass_in[sweep, pl.ds(first, count)] = jnp.zeros(
                        (count, group, block), jnp.float32
                    )
    for source in (-1, 1):
        @pl.when(jnp.logical_not(exists(source)))
        def _(source=source):
            for r in range(local):
                for spot in range(group):
                    dots[r, (1 + source) * group + spot] = jnp.zeros((block, block), jnp.float32)

    small_loads[0].wait()
    pl.semaphore_wait(
        barrier, len(others) + jnp.int32(has_far) + jnp.int32(has_near)
    )
    send_own(0, lambda place: desc_ref.at[place])
    for load in small_loads[1:]:
        load.wait()
    weight_load.wait()

    lanes = lax.broadcasted_iota(jnp.int32, (1, block), 1)
    rows_at = lax.broadcasted_iota(jnp.int32, (block, 1), 0)
    head_of = lax.broadcasted_iota(jnp.int32, (1, width), 1) // head_dim
    own_kpt = [kpt_ref[(img * blk_count + blk) * local + r] for r in range(local)]
    near_ids = [
        [jnp.clip(cov_ref[r, t] - first_block, 0, 3 * group - 1) for t in range(tiles)]
        for r in range(local)
    ]
    limits = [
        [
            jnp.where(t < count_ref[r], kpt_ref[jnp.clip(cov_ref[r, t], 0, kpt_ref.shape[0] - 1)], 0)
            for t in range(tiles)
        ]
        for r in range(local)
    ]
    biases = [
        [jnp.where(lanes < limits[r][t], 0.0, DEAD) for t in range(tiles)] for r in range(local)
    ]
    for r in range(local):
        for spot in range(3 * group):
            limit = 0
            for t in range(tiles):
                limit = jnp.where(near_ids[r][t] == spot, limits[r][t], limit)
            slot_limit[r, spot] = limit

    own = desc_ref[...].reshape(local * block, width)
    query = jnp.dot(own, weight(0), preferred_element_type=jnp.float32).astype(jnp.bfloat16)
    for r in range(local):
        q = query[r * block : (r + 1) * block]
        turned = lax.dot_general(
            jnp.concatenate(
                [jnp.where(head_of == head, q, jnp.zeros_like(q)) for head in range(HEADS)], axis=0
            ),
            weight(1),
            (((1,), (1,)), ((), ())),
            preferred_element_type=jnp.float32,
        )
        spans[r] = (turned * (math.log2(math.e) / math.sqrt(head_dim))).astype(jnp.bfloat16)
    value_turned[...] = weight(2).T
    columns = deep // width
    for column in range(columns):
        merged[:, pl.ds(column * width, width)] = jnp.dot(
            own, merge_part(0, column), preferred_element_type=jnp.float32
        )
    places_at = lax.broadcasted_iota(jnp.int32, (block, block), 0)
    step_heads = 2 if HEADS % 2 == 0 else 1

    def attend(rows, spots, first=False):
        values = lax.dot_general(
            value_turned[...], rows, (((1,), (1,)), ((), ())), preferred_element_type=jnp.float32
        ).astype(jnp.bfloat16)
        lives = [[places_at < slot_limit[r, spot] for spot in spots] for r in range(local)]
        chains = [(r, base) for r in range(local) for base in range(0, HEADS, step_heads)]

        def compare(chain):
            r, base = chain
            logits = lax.dot_general(
                rows,
                spans[r, pl.ds(base * block, step_heads * block)],
                (((1,), (1,)), ((), ())),
                preferred_element_type=jnp.float32,
            )
            tops = []
            for head in range(step_heads):
                top = None
                for place, alive in enumerate(lives[r]):
                    where_to = (pl.ds(place * block, block), pl.ds(head * block, block))
                    part = jnp.where(
                        alive,
                        logits[
                            place * block : (place + 1) * block,
                            head * block : (head + 1) * block,
                        ],
                        DEAD,
                    )
                    logit_ref[r, base // step_heads, where_to[0], where_to[1]] = part
                    top = part if top is None else jnp.maximum(top, part)
                tops.append(jnp.max(top, axis=0, keepdims=True))
            return tops

        def soften(chain, logits):
            r, base = chain
            weights = []
            scales = []
            for head in range(step_heads):
                where_to = pl.ds(base + head, 1)
                parts = [
                    logit_ref[
                        r,
                        base // step_heads,
                        pl.ds(place * block, block),
                        pl.ds(head * block, block),
                    ]
                    for place in range(len(spots))
                ]
                top = logits[head]
                if not first:
                    old = top_ref[r, where_to, :]
                    top = jnp.maximum(top, old)
                    scales.append(jnp.exp2(old - top))
                parts = [jnp.exp2(part - top) for part in parts]
                total = jnp.sum(functools.reduce(jnp.add, parts), axis=0, keepdims=True)
                if not first:
                    total = total + sum_ref[r, where_to, :] * scales[head]
                top_ref[r, where_to, :] = top
                sum_ref[r, where_to, :] = total
                weights.append(
                    jnp.concatenate([part.astype(jnp.bfloat16) for part in parts], axis=0)
                )
            return jnp.concatenate(weights, axis=1), scales

        def blend(chain, weights, scales):
            r, base = chain
            out = jnp.dot(
                values[base * head_dim : (base + step_heads) * head_dim],
                weights,
                preferred_element_type=jnp.float32,
            )
            for head in range(step_heads):
                where_to = pl.ds((base + head) * head_dim, head_dim)
                mix = out[
                    head * head_dim : (head + 1) * head_dim, head * block : (head + 1) * block
                ]
                if not first:
                    mix = mix + mix_ref[r, where_to, :] * scales[head]
                mix_ref[r, where_to, :] = mix

        compared = [compare(chain) for chain in chains]
        softened = [soften(chain, logits) for chain, logits in zip(chains, compared)]
        for chain, soft in zip(chains, softened):
            blend(chain, *soft)

    def attend_near(spots):
        attend(jnp.concatenate([near_desc[spot] for spot in spots], axis=0), spots)

    attend(own, [slot_of(1, blk, place) for place in range(local)], first=True)
    collect(0, attend_near)

    message = jnp.concatenate(
        [
            jnp.concatenate(
                [
                    mix_ref[r, pl.ds(head * head_dim, head_dim), :]
                    * (1.0 / sum_ref[r, pl.ds(head, 1), :])
                    for head in range(HEADS)
                ],
                axis=0,
            )
            for r in range(local)
        ],
        axis=1,
    ).astype(jnp.bfloat16)
    refined = desc_ref[...].reshape(local * block, width).astype(jnp.float32)
    for column in range(columns):
        hidden = jnp.maximum(
            merged[:, pl.ds(column * width, width)]
            + lax.dot_general(
                message,
                merge_part(1, column),
                (((0,), (0,)), ((), ())),
                preferred_element_type=jnp.float32,
            ),
            0.0,
        ).astype(jnp.bfloat16)
        refined = refined + jnp.dot(
            hidden,
            weights_ref[pl.ds(starts[3] + column * width, width), :],
            preferred_element_type=jnp.float32,
        )
    refined = refined.astype(jnp.bfloat16)
    near_ref[pl.ds(slot_of(1, blk, 0), local)] = refined.reshape(local, block, width)
    send_own(1, lambda place: near_ref.at[slot_of(1, blk, place)])

    mine = refined * jnp.asarray(1.0 / math.sqrt(width), jnp.bfloat16)

    def multiply(spots):
        theirs = jnp.concatenate([near_ref[spot] for spot in spots], axis=0)
        out = lax.dot_general(
            mine, theirs, (((1,), (1,)), ((), ())), preferred_element_type=jnp.float32
        )
        for r in range(local):
            for place, spot in enumerate(spots):
                dots[r, spot] = LOG2E * out[
                    r * block : (r + 1) * block, place * block : (place + 1) * block
                ]

    multiply([slot_of(1, blk, place) for place in range(local)])
    collect(1, multiply)

    dust = dust_in[0]
    dust2 = dust * LOG2E
    row_live = [rows_at < own_kpt[r] for r in range(local)]
    row_bias = [jnp.where(row_live[r], 0.0, DEAD) for r in range(local)]

    slots = lax.broadcasted_iota(jnp.int32, (group, 1), 0)
    pots = [jnp.zeros((group, block), jnp.float32)] * 3

    def mass_start(sweep, shift, member):
        first, count = mass_at(-shift, blk)
        pltpu.make_async_remote_copy(
            src_ref=acc.at[sweep, pl.ds(max(0, shift), count)],
            dst_ref=mass_in.at[sweep, pl.ds(first, count)],
            send_sem=mass_ssem.at[0],
            recv_sem=mass_rsem.at[sweep],
            device_id=(img + shift, member),
            device_id_type=MESH,
        ).start()

    def mass_wait(sweep):
        for below in range(3):
            for above in range(3):
                count = 3 * len(others)
                for reach in (below, above):
                    count += sum((3 - step) * blk_count for step in range(1, reach + 1))

                @pl.when(
                    jnp.logical_and(
                        jnp.minimum(img, 2) == below,
                        jnp.minimum(img_count - 1 - img, 2) == above,
                    )
                )
                def _(count=count):
                    if sweep is None:
                        here = mass_in.at[:, pl.ds(0, count)]
                    else:
                        here = mass_in.at[sweep, pl.ds(0, count)]
                    copy = pltpu.make_async_remote_copy(
                        src_ref=here,
                        dst_ref=here,
                        send_sem=mass_ssem.at[0],
                        recv_sem=mass_rsem.at[0 if sweep is None else sweep],
                        device_id=(img, others[0]),
                        device_id_type=MESH,
                    )
                    if sweep is None:
                        copy.wait_send()
                    else:
                        copy.wait_recv()

    inner = jnp.logical_and(exists(-2), exists(2))

    def each_partner(body):
        def run(shift):
            for member in others if shift == 0 else range(blk_count):
                body(shift, member)

        @pl.when(inner)
        def _():
            for shift in (-1, 1, -2, 2, 0):
                run(shift)

        @pl.when(jnp.logical_not(inner))
        def _():
            for shift in (-1, 1, -2, 2):
                pl.when(exists(shift))(lambda shift=shift: run(shift))
            run(0)

    row_pots = [None] * local
    for sweep in range(ITERS):
        spread = [jnp.zeros((group, block), jnp.float32)] * 3
        for r in range(local):
            top = None
            for t in range(tiles):
                if sweep == 0:
                    moved = dots[r, near_ids[r][t]] + (row_bias[r] + biases[r][t])
                    scores[r, t] = moved
                else:
                    moved = scores[r, t] + pot[pl.ds(near_ids[r][t], 1), :]
                    shifted[r, t] = moved
                top = moved if t == 0 else jnp.maximum(top, moved)
            held = scores if sweep == 0 else shifted
            top = jnp.maximum(jnp.max(top, axis=1, keepdims=True), dust2)
            terms = [jnp.exp2(held[r, t] - top) for t in range(tiles)]
            total = functools.reduce(jnp.add, terms)
            total = jnp.sum(total, axis=1, keepdims=True) + jnp.exp2(dust2 - top)
            row_pots[r] = -(top + jnp.log2(total))
            inverse = 1.0 / total
            for t in range(tiles):
                mass = jnp.sum(terms[t] * inverse, axis=0, keepdims=True)
                for section in range(3):
                    hit = slots == near_ids[r][t] - section * group
                    spread[section] = spread[section] + jnp.where(hit, mass, 0.0)
        for section in range(3):
            acc[sweep, section] = spread[section]
        each_partner(lambda shift, member: mass_start(sweep, shift, member))
        if sweep == 0:
            drain(0)
            drain(1)
        if sweep == ITERS - 1:
            for r in range(local):
                row = jnp.broadcast_to(row_pots[r] * LN2, (block, block))
                row = jnp.sum(jnp.where(rows_at == lanes, row, 0.0), axis=0, keepdims=True)
                tail_ref[pl.ds(local * tiles + r, 1), :] = jnp.where(lanes < own_kpt[r], dust + row, 0.0)
                for t in range(tiles):
                    scores[r, t] = (scores[r, t] + row_pots[r]) * LN2
        sums = list(spread)
        mass_wait(sweep)
        for source in range(-2, 3):
            for member in others if source == 0 else range(blk_count):
                for section in range(max(0, source), 3 + min(0, source)):
                    first, _ = mass_at(source, member)
                    sums[section] = sums[section] + mass_in[
                        sweep, first + section - max(0, source)
                    ]
        for section in range(3):
            pots[section] = pots[section] - jnp.log2(
                sums[section] + jnp.exp2(dust2 + pots[section])
            )
            pot[pl.ds(section * group, group), :] = (
                pots[section] * LN2 if sweep == ITERS - 1 else pots[section]
            )

    for r in range(local):
        for t in range(tiles):
            tail_ref[pl.ds(r * tiles + t, 1), :] = pot[pl.ds(near_ids[r][t], 1), :]
        mine = pot[pl.ds(group + blk * local + r, 1), :]
        tail_ref[pl.ds(local * (tiles + 1) + r, 1), :] = jnp.where(lanes < own_kpt[r], dust + mine, 0.0)
    mass_wait(None)


def finish(base_ref, tail_ref, plan_out, row_out, col_out, made, out_sem, end_sem):
    local, tiles = base_ref.shape[:2]
    places = [(r, t) for r in range(local) for t in range(tiles)]

    def put(r, t):
        return pltpu.make_async_copy(made.at[r, t], plan_out.at[r, t], out_sem)

    ends = [
        pltpu.make_async_copy(
            tail_ref.at[pl.ds(local * (tiles + step), local)], target, end_sem.at[step]
        )
        for step, target in enumerate((row_out, col_out))
    ]
    for end in ends:
        end.start()
    for r, t in places:
        base = base_ref[r, t]
        out = base + tail_ref[pl.ds(r * tiles + t, 1), :]
        made[r, t] = jnp.where(base > 0.1 * DEAD, out, 0.0)
        put(r, t).start()
    for end in ends:
        end.wait()
    pltpu.make_async_copy(made, plan_out, out_sem).wait()


def on_device(
    img_count,
    blk_count,
    descriptors,
    covisible,
    tile_counts,
    keypoints,
    query_weight,
    key_weight,
    value_weight,
    merge_weight,
    output_weight,
    dustbin,
):
    local, block, width = descriptors.shape
    tiles = covisible.shape[1]
    group = local * blk_count
    near = 3 * group
    most = max(local * (blk_count - 1), (local - 1) * blk_count + 1, blk_count, local)
    pace = 2 if HEADS % 2 == 0 else 1
    weight_rows = (
        3 * width
        + output_weight.shape[0]
        + merge_weight.shape[0] * (merge_weight.shape[1] // width)
    )
    vmem = pl.BlockSpec(memory_space=pltpu.VMEM)
    hbm = pl.BlockSpec(memory_space=pltpu.HBM)
    dma = pltpu.SemaphoreType.DMA
    half = jnp.bfloat16
    full = jnp.float32
    base, tail = pl.pallas_call(
        functools.partial(kernel, img_count, blk_count),
        out_shape=(
            pltpu.VMEM((local, tiles, block, block), full),
            pltpu.VMEM((local * (tiles + 2), block), full),
        ),
        in_specs=[hbm] * 9 + [pl.BlockSpec(memory_space=pltpu.SMEM)],
        out_specs=(vmem, vmem),
        scratch_shapes=[
            pltpu.VMEM(descriptors.shape, half),
            pltpu.SMEM(covisible.shape, jnp.int32),
            pltpu.SMEM(tile_counts.shape, jnp.int32),
            pltpu.SMEM(keypoints.shape, jnp.int32),
            pltpu.SMEM(dustbin.shape, full),
            pltpu.VMEM((weight_rows, width), half),
            dma((6,)),
            pltpu.VMEM((near, block, width), half),
            pltpu.VMEM((near, block, width), half),
            pltpu.VMEM(value_weight.shape, half),
            pltpu.VMEM((local, HEADS * block, width), half),
            pltpu.VMEM((local * block, merge_weight.shape[1]), full),
            pltpu.SMEM((local, near), jnp.int32),
            pltpu.VMEM((local, HEADS, block), full),
            pltpu.VMEM((local, HEADS, block), full),
            pltpu.VMEM((local, width, block), full),
            pltpu.VMEM((local, HEADS // pace, most * block, pace * block), full),
            pltpu.VMEM((local, near, block, block), full),
            pltpu.VMEM((local, tiles, block, block), full),
            pltpu.VMEM((ITERS, 3, group, block), full),
            pltpu.VMEM((ITERS, 9 * blk_count, group, block), full),
            pltpu.VMEM((near, block), full),
            dma((2,)),
            dma((2,)),
            dma((2, 2, local)),
            dma((2, 2, local)),
            dma((1,)),
            dma((ITERS,)),
        ],
        compiler_params=pltpu.CompilerParams(
            collective_id=0, has_side_effects=True, vmem_limit_bytes=VMEM_BYTES
        ),
    )(
        *(
            pltpu.with_memory_space_constraint(x, pltpu.HBM)
            for x in (
                descriptors,
                covisible,
                tile_counts,
                keypoints,
                query_weight,
                key_weight,
                value_weight,
                merge_weight,
                output_weight,
            )
        ),
        dustbin,
    )
    return pl.pallas_call(
        finish,
        out_shape=(
            jax.ShapeDtypeStruct(base.shape, full),
            jax.ShapeDtypeStruct((local, block), full),
            jax.ShapeDtypeStruct((local, block), full),
        ),
        in_specs=[vmem, vmem],
        out_specs=(hbm, hbm, hbm),
        scratch_shapes=[
            pltpu.VMEM(base.shape, full),
            dma,
            dma((2,)),
        ],
        compiler_params=pltpu.CompilerParams(vmem_limit_bytes=VMEM_BYTES),
    )(*(pltpu.with_memory_space_constraint(x, pltpu.VMEM) for x in (base, tail)))


def solution(mesh):
    in_specs = (
        P(("img", "blk"), None, None),
        P(("img", "blk"), None),
        P(("img", "blk")),
        P(),
        P(),
        P(),
        P(),
        P(),
        P(),
        P(),
    )
    out_specs = (
        P(("img", "blk"), None, None, None),
        P(("img", "blk"), None),
        P(("img", "blk"), None),
    )
    return jax.shard_map(
        functools.partial(on_device, mesh.shape["img"], mesh.shape["blk"]),
        mesh=mesh,
        in_specs=in_specs,
        out_specs=out_specs,
        check_vma=False,
    )
```
